128 devices in a mesh: gx: 4 (over y), gy: 4 (over x), gz: 8 (over z, core).
Axes of the slice: x: 4, y: 4, z: 4, core: 2. Of those that a mesh axis runs over, the one named last changes fastest.
Arguments:
- hidden: bfloat16 [16384, 2, 4096], P(('gx', 'gy', 'gz')), may hold values from -6 to 6
- norm_gain: float32 [4096], replicated, may hold values from 0.25 to 1.75
- prompt_of: int32 [16384], P(('gx', 'gy', 'gz')), may hold values from 0 to 1023, as said below
- lengths: int32 [16384], P(('gx', 'gy', 'gz')), may hold values from 1 to 2
- reward_level: int32 [16384], P(('gx', 'gy', 'gz')), may hold values from 0 to 15
Outputs:
- weighted: bfloat16 [16384, 2, 4096], P(('gx', 'gy', 'gz'))
- advantages: float32 [16384], P(('gx', 'gy', 'gz'))
The draws below stay inside these ranges and needn't reach their ends.
Inputs may be any that keep to these rules, and one draw needn't show every extreme that they name: `prompt_of`: each of the 1024 prompts has exactly 16 completions; prompt p is owned by the device p // 8 in mesh order; the completions of one device include at most 2 whose prompts one owner holds, and exactly 2 for some owner.
All inputs are finite; a program needn't handle non-finite values.
Results may differ from the reference program's by a relative error of at most 0.0085.
Values may be sent and summed in bfloat16 or wider, within the bound.
A program may use at most 64 MiB of HBM per device.

```python
import jax
import jax.numpy as jnp
from jax import lax

D = 4096
G = 16
P_DEV = 8
W = 2
OWNERS = 128
COMP_DEV = 128
SLOTS = 2
COMPLETIONS = 16384
PROMPTS = 1024


def regroup_plan(key):
    plan_key = jax.random.fold_in(key, 7301)
    key_offsets, key_shift, key_member, key_tiebreak = jax.random.split(plan_key, 4)
    chosen = jax.random.permutation(key_offsets, OWNERS)
    member_index = jnp.arange(COMP_DEV, dtype=jnp.int32)
    spread_index = jnp.where(member_index < SLOTS, 0, 1 + (member_index - SLOTS) % (OWNERS - 1))
    offsets = chosen[spread_index]
    owner_shift = jax.random.permutation(key_shift, OWNERS)

    def member_order(member_key):
        return jax.random.permutation(member_key, COMP_DEV)
    member_perm = jax.vmap(member_order)(jax.random.split(key_member, OWNERS))
    target_device = (owner_shift[:, None] + offsets[member_perm]) % OWNERS
    prompt_ids = jnp.arange(OWNERS, dtype=jnp.int32)[:, None] * P_DEV + jnp.arange(COMP_DEV, dtype=jnp.int32)[None, :] // G
    tiebreak = jax.random.permutation(key_tiebreak, COMPLETIONS)
    scores = target_device.reshape(-1) * COMPLETIONS + tiebreak
    arranged = jnp.argsort(scores)
    return prompt_ids.reshape(-1)[arranged].astype(jnp.int32)


def draw_prompt_of(key, part):
    return regroup_plan(key)


def draw_reward_level(key, part):
    prompt_ids = regroup_plan(key)
    key_base, key_spread, key_jitter = jax.random.split(jax.random.fold_in(key, 911), 3)
    base_level = jax.random.randint(key_base, (PROMPTS,), 0, 9)
    spread = jax.random.randint(key_spread, (PROMPTS,), 1, 9)
    jitter = jax.random.randint(key_jitter, (COMPLETIONS,), 0, 65536) % spread[prompt_ids]
    return (base_level[prompt_ids] + jitter).astype(jnp.int32)


def set_ends(values, key, smallest, high):
    spot = [jax.random.randint(jax.random.fold_in(key, axis), (), 0, length) for axis, length in enumerate(values.shape)]
    widest = values.shape.index(max(values.shape))
    neighbour = spot[:widest] + [(spot[widest] + 1) % values.shape[widest]] + spot[widest + 1:]
    return values.at[tuple(spot)].set(smallest).at[tuple(neighbour)].set(high)


def block_scale(key, dims, cuts, smallest, high):
    factor_of, own = 1.0, jax.random.fold_in(key, 6)
    for position, blocks in cuts:
        heights = jnp.exp(jax.random.uniform(jax.random.fold_in(own, position), (blocks,), jnp.float32, smallest / len(cuts), high / len(cuts)))
        factor_of = factor_of * jnp.repeat(heights, dims[position] // blocks).reshape([-1 if axis == position else 1 for axis in range(len(dims))])
    return factor_of


def centred(key, shape, scale, reach, pieces=(), kind=jnp.bfloat16):
    gain = block_scale(key, shape, pieces, -0.22, 0.18) if pieces else 1.0
    result = jax.random.normal(key, shape, jnp.float32) * scale * gain
    return jnp.minimum(jnp.maximum(result, -reach), reach).astype(kind)


def setup_inputs(seed: int = 0) -> dict:
    seeds = jax.random.split(jax.random.key(seed), 6)
    hidden = centred(seeds[0], (COMPLETIONS, W, D), 1.0, 6.0, ((0, 128),))
    norm_gain = jnp.clip(1.0 + 0.15 * jax.random.normal(seeds[1], (D,), jnp.float32), 0.25, 1.75)
    prompt_of = draw_prompt_of(jax.random.fold_in(seeds[5], 71), 0)
    lengths = set_ends(jax.random.randint(seeds[3], (COMPLETIONS,), 1, W + 1), jax.random.fold_in(seeds[3], 1), 1, W).astype(jnp.int32)
    reward_level = draw_reward_level(jax.random.fold_in(seeds[5], 71), 0)
    return dict(hidden=hidden, norm_gain=norm_gain, prompt_of=prompt_of, lengths=lengths, reward_level=reward_level)


norm_eps = 1e-05

def normalize(block, norm_gain):
    values = block.astype(jnp.float32)
    meansq = lax.optimization_barrier(jnp.mean(values * values, axis=-1, keepdims=True))
    return (values * lax.rsqrt(meansq + norm_eps) * norm_gain.astype(jnp.float32)).astype(jnp.bfloat16)

def reference(hidden, norm_gain, prompt_of, lengths, reward_level):
    blocks = hidden.reshape(OWNERS, COMP_DEV, W, D)

    def norm_block(block):
        return normalize(block, norm_gain)
    normed = lax.map(norm_block, blocks).reshape(COMPLETIONS, W, D)
    ordering = jnp.argsort(prompt_of, stable=True).astype(jnp.int32)
    normed = normed[ordering]
    levels = reward_level[ordering].astype(jnp.float32).reshape(PROMPTS, G)
    average = lax.optimization_barrier(jnp.mean(levels, axis=1, keepdims=True))
    centered = levels - average
    spread = jnp.sqrt(lax.optimization_barrier(jnp.mean(centered * centered, axis=1, keepdims=True)))
    advantages = (centered / jnp.maximum(spread, 1.0)).reshape(COMPLETIONS)
    lengths_sorted = lengths[ordering]
    tokens_at = jnp.arange(W, dtype=jnp.int32)
    weight = jnp.where(tokens_at[None, :] < lengths_sorted[:, None], advantages[:, None] / lengths_sorted[:, None].astype(jnp.float32), 0.0)

    def scale_block(pair):
        block, block_weight = pair
        return (block.astype(jnp.float32) * block_weight[:, :, None]).astype(jnp.bfloat16)
    weighted = lax.map(scale_block, (normed.reshape(OWNERS, COMP_DEV, W, D), weight.reshape(OWNERS, COMP_DEV, W)))
    return (weighted.reshape(COMPLETIONS, W, D), advantages)
```

```python
import functools

import jax
import jax.numpy as jnp
from jax import lax
from jax.experimental import pallas as pl
from jax.experimental.pallas import tpu as pltpu
from jax.sharding import PartitionSpec as P

MESH = pl.DeviceIdType.MESH
AXES = ("gx", "gy", "gz")
N = 128
G = 16
OWN = 8
SLOTS = 2
STRIDE = 37
norm_eps = 1e-05

NT = (((1,), (1,)), ((), ()))
NN = (((1,), (0,)), ((), ()))


def dot(a, b, dims, exact=False):
    if exact:
        return lax.dot_general(a, b, dims, precision=lax.Precision.HIGHEST,
                               preferred_element_type=jnp.float32)
    return lax.dot_general(a.astype(jnp.bfloat16), b.astype(jnp.bfloat16), dims,
                           preferred_element_type=jnp.float32)


def coords(p):
    return (p // 32, lax.rem(p // 8, 4), lax.rem(p, 8))


def shifted(me, o, sign):
    mx, my, mz, mc = me // 32, lax.rem(me // 8, 4), lax.rem(me // 2, 4), lax.rem(me, 2)
    ox, oy, oz, oc = o // 32, lax.rem(o // 8, 4), lax.rem(o // 2, 4), lax.rem(o, 2)
    x, y = lax.rem(mx + sign * ox + 4, 4), lax.rem(my + sign * oy + 4, 4)
    z, c = lax.rem(mz + sign * oz + 4, 4), lax.rem(mc + oc, 2)
    return x * 32 + y * 8 + z * 2 + c


def exchange(hidden, gain, prompt_of, lengths, reward, rows_out, table_out, adv_out,
             hbuf, gbuf, tab, itab, stab, meta, meta_in, send, recv, wtab, wsm, outv,
             in_sem, tab_sem, meta_send, meta_recv, send_sem, recv_sem, out_sem):
    me = lax.axis_index("gx") * 32 + lax.axis_index("gy") * 8 + lax.axis_index("gz")
    barrier = pltpu.get_barrier_semaphore()

    def greet(i, _):
        pl.semaphore_signal(barrier, inc=1, device_id=coords(lax.rem(me + i, N)), device_id_type=MESH)
        return 0
    lax.fori_loop(1, N, greet, 0)

    fetch_rows = pltpu.make_async_copy(hidden, hbuf, in_sem.at[0])
    fetch_gain = pltpu.make_async_copy(gain, gbuf, in_sem.at[1])
    fetch_tab = [pltpu.make_async_copy(ref, tab.at[pl.ds(k, 1)], in_sem.at[2 + k])
                 for k, ref in enumerate((prompt_of, lengths, reward))]
    for copy in fetch_tab:
        copy.start()
    fetch_rows.start()
    fetch_gain.start()
    for copy in fetch_tab:
        copy.wait()

    rows = lax.broadcasted_iota(jnp.int32, (N, N), 0)
    lanes = lax.broadcasted_iota(jnp.int32, (N, N), 1)
    before = jnp.where(rows < lanes, 1.0, 0.0)
    row8 = lax.broadcasted_iota(jnp.int32, (8, N), 0)
    lane8 = lax.broadcasted_iota(jnp.int32, (8, N), 1)

    prompt, length, level = tab[0:1], tab[1:2], tab[2:3]
    owner, label = prompt // OWN, lax.rem(prompt, OWN) + 1
    mine = owner == rows
    held = jnp.where(mine, 1.0, 0.0)
    earlier = dot(held, before, NN)
    slot0 = jnp.where(mine & (earlier < 0.5), 1.0, 0.0)
    slot1 = jnp.where(mine & (earlier == 1.0), 1.0, 0.0)
    pick = (dot(jnp.where(row8 == 0, lane8, 0).astype(jnp.float32), slot0, NT)
            + dot(jnp.where(row8 == 1, lane8, 0).astype(jnp.float32), slot1, NT))
    itab[...] = pick.astype(jnp.int32)
    to_scalar = pltpu.make_async_copy(itab, stab, tab_sem.at[0])
    to_scalar.start()
    zero = jnp.zeros((N, N), jnp.int32)
    told = jnp.where(rows == 0, label, jnp.where(rows == 1, level, jnp.where(rows == 2, length, zero)))
    told1 = jnp.where(rows == 3, label, jnp.where(rows == 4, level, jnp.where(rows == 5, length, zero)))
    meta[...] = (dot(slot0, told.astype(jnp.float32), NT) + dot(slot1, told1.astype(jnp.float32), NT)).astype(jnp.int32)
    to_scalar.wait()
    fetch_rows.wait()

    pl.semaphore_wait(barrier, N - 1)

    own_meta = pltpu.make_async_copy(meta.at[pl.ds(me, 1)], meta_in.at[pl.ds(me, 1)], meta_recv)
    own_meta.start()

    def tell(i, _):
        to = lax.rem(me + i, N)
        pltpu.make_async_remote_copy(
            src_ref=meta.at[pl.ds(to, 1)], dst_ref=meta_in.at[pl.ds(me, 1)], send_sem=meta_send, recv_sem=meta_recv,
            device_id=coords(to), device_id_type=MESH).start()
        return 0
    lax.fori_loop(1, N, tell, 0)

    def pack(i):
        to = shifted(me, lax.rem(i * STRIDE, N), 1)
        for s in range(SLOTS):
            send[to, s] = hbuf[jnp.clip(stab[s, to], 0, N - 1)]

    def ship(i):
        o = lax.rem(i * STRIDE, N)
        to = shifted(me, o, 1)
        pltpu.make_async_remote_copy(
            src_ref=send.at[to], dst_ref=recv.at[me], send_sem=send_sem, recv_sem=recv_sem.at[o],
            device_id=coords(to), device_id_type=MESH).start()

    lead = 4
    for i in range(lead):
        pack(i)

    own = pltpu.make_async_copy(send.at[me], recv.at[me], recv_sem.at[0])

    def step(i, _):
        pack(i + lead)
        ship(i)
        return 0
    pack(lead)
    own.start()
    lax.fori_loop(1, N - lead, step, 0)

    def last(i, _):
        ship(i)
        return 0
    lax.fori_loop(N - lead, N, last, 0)

    pltpu.make_async_copy(meta_in, meta_in, meta_recv).wait()
    told_in = meta_in[...].astype(jnp.float32)
    unit = jnp.where(row8 == lane8, 1.0, 0.0)
    by_source = dot(unit, told_in, NT)
    label0, label1 = by_source[0:1], by_source[3:4]
    group = (rows // G + 1).astype(jnp.float32)
    rank = lax.rem(rows, G).astype(jnp.float32)
    in0, in1 = jnp.where(label0 == group, 1.0, 0.0), jnp.where(label1 == group, 1.0, 0.0)
    ahead = dot(in0 + in1, before, NN)
    take0 = jnp.where((in0 > 0.5) & (ahead == rank), 1.0, 0.0)
    take1 = jnp.where((in1 > 0.5) & (ahead + in0 == rank), 1.0, 0.0)
    lanef = lane8.astype(jnp.float32)
    facts0 = jnp.where(row8 == 0, by_source[1:2], jnp.where(row8 == 1, by_source[2:3], jnp.where(row8 == 2, 2 * lane8, 0).astype(jnp.float32)))
    facts1 = jnp.where(row8 == 0, by_source[4:5], jnp.where(row8 == 1, by_source[5:6], jnp.where(row8 == 2, 2 * lane8 + 1, 0).astype(jnp.float32)))
    facts = dot(facts0, take0, NT) + dot(facts1, take1, NT)
    same = jnp.where(rows // G == lanes // G, 1.0, 0.0)
    mean = dot(facts, same, NN) * (1.0 / G)
    centred = facts - mean
    spread = jnp.sqrt(dot(centred * centred, same, NN, exact=True) * (1.0 / G))
    adv = centred[0:1] / jnp.maximum(spread[0:1], 1.0)
    count = facts[1:2]
    weight = adv / count
    wrows = jnp.where(row8 == 0, weight, jnp.where((row8 == 1) & (count > 1.5), weight, 0.0))
    wtab[0] = dot(wrows, take0, NN, exact=True)
    wtab[1] = dot(wrows, take1, NN, exact=True)
    weights_out = pltpu.make_async_copy(wtab, wsm, tab_sem.at[1])
    weights_out.start()
    table_out[...] = facts[2:3].astype(jnp.int32)
    adv_out[...] = adv
    weights_out.wait()
    fetch_gain.wait()

    token = lax.broadcasted_iota(jnp.int32, (2, 1), 0)
    gains = gbuf[...]

    def settle(i, _):
        o = lax.rem(i * STRIDE, N)
        src = shifted(me, o, -1)
        pltpu.make_async_copy(recv.at[src], recv.at[src], recv_sem.at[o]).wait()
        for s in range(SLOTS):
            x = recv[src, s].astype(jnp.float32)
            meansq = jnp.mean(x * x, axis=-1, keepdims=True)
            y = (x * lax.rsqrt(meansq + norm_eps) * gains).astype(jnp.bfloat16)
            w = jnp.where(token == 0, wsm[s, 0, src], wsm[s, 1, src])
            outv[src, s] = (y.astype(jnp.float32) * w).astype(jnp.bfloat16)
        return 0
    lax.fori_loop(0, N, settle, 0)
    put = pltpu.make_async_copy(outv, rows_out, out_sem)
    put.start()

    pltpu.make_async_copy(meta.at[pl.ds(0, N - 1)], meta.at[pl.ds(0, N - 1)], meta_send).wait()
    pltpu.make_async_copy(send.at[pl.ds(0, N - 1)], send.at[pl.ds(0, N - 1)], send_sem).wait()
    put.wait()


def arrange(table, adv_in, rows_in, out, adv_out, buf, in_sem, out_sem):
    CH = 16

    def load(q, _):
        pltpu.make_async_copy(rows_in.at[table[0, q]], buf.at[q], in_sem.at[q // CH]).start()
        return 0
    lax.fori_loop(0, N, load, 0)
    adv_out[...] = adv_in[...]
    for c in range(N // CH):
        part = pl.ds(c * CH, CH)
        pltpu.make_async_copy(buf.at[part], buf.at[part], in_sem.at[c]).wait()
        pltpu.make_async_copy(buf.at[part], out.at[part], out_sem).start()
    pltpu.make_async_copy(buf, buf, out_sem).wait()


def on_device(hidden, norm_gain, prompt_of, lengths, reward_level):
    count, window, features = hidden.shape
    bf16, f32, i32 = jnp.bfloat16, jnp.float32, jnp.int32
    any_space = pl.BlockSpec(memory_space=pl.ANY)
    vmem = pl.BlockSpec(memory_space=pltpu.VMEM)
    dma = pltpu.SemaphoreType.DMA
    rows, table, adv = pl.pallas_call(
        exchange,
        out_shape=(jax.ShapeDtypeStruct((N, SLOTS, window, features), bf16),
                   jax.ShapeDtypeStruct((1, N), i32), jax.ShapeDtypeStruct((1, N), f32)),
        in_specs=[any_space] * 5,
        out_specs=(any_space, vmem, vmem),
        scratch_shapes=[
            pltpu.VMEM((N, window, features), bf16), pltpu.VMEM((1, features), f32),
            pltpu.VMEM((8, N), i32), pltpu.VMEM((8, N), i32), pltpu.SMEM((8, N), i32),
            pltpu.VMEM((N, N), i32), pltpu.VMEM((N, N), i32),
            pltpu.VMEM((N, SLOTS, window, features), bf16), pltpu.VMEM((N, SLOTS, window, features), bf16),
            pltpu.VMEM((SLOTS, 8, N), f32), pltpu.SMEM((SLOTS, 8, N), f32),
            pltpu.VMEM((N, SLOTS, window, features), bf16),
            dma((5,)), dma((2,)), dma, dma, dma, dma((N,)), dma],
        compiler_params=pltpu.CompilerParams(collective_id=0, has_side_effects=True),
    )(hidden, norm_gain.reshape(1, features), prompt_of.reshape(1, N), lengths.reshape(1, N), reward_level.reshape(1, N))
    out, adv = pl.pallas_call(
        arrange,
        out_shape=(jax.ShapeDtypeStruct((N, window, features), bf16), jax.ShapeDtypeStruct((1, N), f32)),
        in_specs=[pl.BlockSpec(memory_space=pltpu.SMEM), vmem, any_space],
        out_specs=(any_space, vmem),
        scratch_shapes=[pltpu.VMEM((N, window, features), bf16), dma((8,)), dma],
    )(table, adv, rows.reshape(N * SLOTS, window, features))
    return out, adv.reshape(N)


def solution(mesh):
    spec = P(AXES)
    return jax.shard_map(
        on_device, mesh=mesh, in_specs=(P(AXES, None, None), P(), spec, spec, spec),
        out_specs=(P(AXES, None, None), spec), check_vma=False)
```

```python
import functools

import jax
import jax.numpy as jnp
from jax import lax
from jax.experimental import pallas as pl
from jax.experimental.pallas import tpu as pltpu
from jax.sharding import PartitionSpec as P

MESH = pl.DeviceIdType.MESH
AXES = ("gx", "gy", "gz")
N = 128
G = 16
OWN = 8
PIECES = 32
EARLY = 40
LATE = 120
STRIDE = 37
norm_eps = 1e-05

NT = (((1,), (1,)), ((), ()))
NN = (((1,), (0,)), ((), ()))


def dot(a, b, dims, exact=False):
    if exact:
        return lax.dot_general(a, b, dims, precision=lax.Precision.HIGHEST,
                               preferred_element_type=jnp.float32)
    return lax.dot_general(a.astype(jnp.bfloat16), b.astype(jnp.bfloat16), dims,
                           preferred_element_type=jnp.float32)


def coords(p):
    return (p // 32, lax.rem(p // 8, 4), lax.rem(p, 8))


def shifted(me, o, sign):
    mx, my, mz, mc = me // 32, lax.rem(me // 8, 4), lax.rem(me // 2, 4), lax.rem(me, 2)
    ox, oy, oz, oc = o // 32, lax.rem(o // 8, 4), lax.rem(o // 2, 4), lax.rem(o, 2)
    x, y = lax.rem(mx + sign * ox + 4, 4), lax.rem(my + sign * oy + 4, 4)
    z, c = lax.rem(mz + sign * oz + 4, 4), lax.rem(mc + oc, 2)
    return x * 32 + y * 8 + z * 2 + c


def my_place():
    return lax.axis_index("gx") * 32 + lax.axis_index("gy") * 8 + lax.axis_index("gz")


def greet_all(me):
    barrier = pltpu.get_barrier_semaphore()

    def greet(i, _):
        pl.semaphore_signal(barrier, inc=1, device_id=coords(lax.rem(me + i, N)), device_id_type=MESH)
        return 0
    lax.fori_loop(1, N, greet, 0)
    return barrier


def slots_of(owner, rows, before):
    mine = owner == rows
    earlier = dot(jnp.where(mine, 1.0, 0.0), before, NN)
    slot0 = jnp.where(mine & (earlier < 0.5), 1.0, 0.0)
    slot1 = jnp.where(mine & (earlier == 1.0), 1.0, 0.0)
    return slot0, slot1


def bounded(i, n):
    return jnp.clip(i, 0, n - 1)


def scaled(x, gains, w0, w1):
    token = lax.broadcasted_iota(jnp.int32, (2, 1), 0)
    x = x.astype(jnp.float32)
    meansq = jnp.mean(x * x, axis=-1, keepdims=True)
    y = (x * lax.rsqrt(meansq + norm_eps) * gains).astype(jnp.bfloat16)
    return (y.astype(jnp.float32) * jnp.where(token == 0, w0, w1)).astype(jnp.bfloat16)


def row_traffic(me, hbuf, stab, send, recv, send_sem, recv_sem):
    def pack(i):
        to = shifted(me, lax.rem(i * STRIDE, N), 1)
        send[to] = hbuf[bounded(stab[0, to], N)]

    def ship(i):
        o = lax.rem(i * STRIDE, N)
        to = shifted(me, o, 1)
        pltpu.make_async_remote_copy(
            src_ref=send.at[to], dst_ref=recv.at[me], send_sem=send_sem, recv_sem=recv_sem.at[o],
            device_id=coords(to), device_id_type=MESH).start()

    def await_row(i):
        o = lax.rem(i * STRIDE, N)
        src = shifted(me, o, -1)
        pltpu.make_async_copy(recv.at[src], recv.at[src], recv_sem.at[o]).wait()
        return src
    own = pltpu.make_async_copy(send.at[me], recv.at[me], recv_sem.at[0])
    return pack, ship, await_row, own


def drained(ref, sem):
    part = ref.at[pl.ds(0, N - 1)]
    pltpu.make_async_copy(part, part, sem).wait()


def exchange(hidden, gain, prompt_of, lengths, reward, rows_out, table_out, adv_out, weights_out,
             hbuf, gbuf, tab, itab, stab, jtab, ttab, meta, meta_in, extra, piece_in, part, part_in, extra_in,
             send, recv, wtab, wsm, outv,
             in_sem, tab_sem, meta_send, meta_recv, piece_send, piece_recv, part_send, part_recv,
             send_sem, recv_sem, out_sem):
    me = my_place()
    barrier = greet_all(me)

    fetch_rows = pltpu.make_async_copy(hidden, hbuf, in_sem.at[0])
    fetch_gain = pltpu.make_async_copy(gain, gbuf, in_sem.at[1])
    fetch_tab = [pltpu.make_async_copy(ref, tab.at[pl.ds(k, 1)], in_sem.at[2 + k])
                 for k, ref in enumerate((prompt_of, lengths, reward))]
    for copy in fetch_tab:
        copy.start()
    fetch_rows.start()
    fetch_gain.start()
    for copy in fetch_tab:
        copy.wait()

    rows = lax.broadcasted_iota(jnp.int32, (N, N), 0)
    lanes = lax.broadcasted_iota(jnp.int32, (N, N), 1)
    before = jnp.where(rows < lanes, 1.0, 0.0)
    row8 = lax.broadcasted_iota(jnp.int32, (8, N), 0)
    lane8 = lax.broadcasted_iota(jnp.int32, (8, N), 1)
    lane1 = lax.broadcasted_iota(jnp.int32, (1, N), 1)
    lanef = lane8.astype(jnp.float32)

    prompt, length, level = tab[0:1], tab[1:2], tab[2:3]
    owner, label = prompt // OWN, lax.rem(prompt, OWN) + 1
    slot0, slot1 = slots_of(owner, rows, before)
    twice = jnp.sum(slot1, axis=0, keepdims=True)
    spare = jnp.sum(twice, axis=1, keepdims=True)
    spare_row = jnp.sum(twice * lane1.astype(jnp.float32), axis=1, keepdims=True)
    spare_to = jnp.where(spare > 0.5, jnp.sum(twice * owner.astype(jnp.float32), axis=1, keepdims=True), -1.0)
    pick = jnp.where(row8 == 0, dot(lanef, slot0, NT), spare_row)
    itab[...] = pick.astype(jnp.int32)
    to_scalar = pltpu.make_async_copy(itab, stab, tab_sem.at[0])
    to_scalar.start()
    zero = jnp.zeros((N, N), jnp.int32)
    told = jnp.where(rows == 0, label, jnp.where(rows == 1, level, jnp.where(rows == 2, length, zero)))
    told1 = jnp.where(rows == 3, label, jnp.where(rows == 4, level, jnp.where(rows == 5, length, zero)))
    meta[...] = (dot(slot0, told.astype(jnp.float32), NT) + dot(slot1, told1.astype(jnp.float32), NT)
                 + jnp.where(lanes == 6, spare_to, jnp.where(lanes == 7, spare, 0.0))).astype(jnp.int32)
    to_scalar.wait()
    fetch_rows.wait()
    extra[...] = hbuf[bounded(stab[1, 0], N)]

    pack, ship, await_row, own = row_traffic(me, hbuf, stab, send, recv, send_sem, recv_sem)
    lead = 4
    for i in range(lead):
        pack(i)
    own_meta = pltpu.make_async_copy(meta.at[pl.ds(me, 1)], meta_in.at[pl.ds(me, 1)], meta_recv)
    own_piece = pltpu.make_async_copy(extra.at[:, pl.ds(0, 128)], piece_in.at[me // 4], piece_recv)
    own_meta.start()
    own_piece.start()

    pl.semaphore_wait(barrier, N - 1)

    def tell(i, _):
        to = lax.rem(me + i, N)
        pltpu.make_async_remote_copy(
            src_ref=meta.at[pl.ds(to, 1)], dst_ref=meta_in.at[pl.ds(me, 1)], send_sem=meta_send, recv_sem=meta_recv,
            device_id=coords(to), device_id_type=MESH).start()
        return 0

    def hand(t, _):
        to = lax.rem(me + 4 * t, N)
        pltpu.make_async_remote_copy(
            src_ref=extra.at[:, pl.ds(pl.multiple_of(t * 128, 128), 128)], dst_ref=piece_in.at[me // 4],
            send_sem=piece_send, recv_sem=piece_recv, device_id=coords(to), device_id_type=MESH).start()
        return 0
    lax.fori_loop(1, N, tell, 0)
    lax.fori_loop(1, PIECES, hand, 0)

    def step(i, _):
        pack(i + lead)
        ship(i)
        return 0
    pack(lead)
    own.start()
    lax.fori_loop(1, EARLY, step, 0)

    pltpu.make_async_copy(meta_in, meta_in, meta_recv).wait()
    told_in = meta_in[...].astype(jnp.float32)
    by_source = dot(jnp.where(row8 == lane8, 1.0, 0.0), told_in, NT)
    label0, label1, to1, spares = by_source[0:1], by_source[3:4], by_source[6:7], by_source[7:8]
    mef = me.astype(jnp.float32)

    passing = jnp.where((to1 == rows.astype(jnp.float32)) & (lax.rem(lane1, 4) == lax.rem(me, 4)), 1.0, 0.0)
    piece_of = dot((lane8 // 4).astype(jnp.float32), passing, NT)
    here = jnp.where(to1 == mef, 1.0, 0.0)
    giver = jnp.sum(here * lane1.astype(jnp.float32), axis=1, keepdims=True)
    jtab[...] = jnp.where(row8 == 0, piece_of, giver).astype(jnp.int32)
    to_scalar = pltpu.make_async_copy(jtab, ttab, tab_sem.at[0])
    to_scalar.start()

    group = (rows // G + 1).astype(jnp.float32)
    rank = lax.rem(rows, G).astype(jnp.float32)
    in0, in1 = jnp.where(label0 == group, 1.0, 0.0), jnp.where(label1 == group, 1.0, 0.0)
    ahead = dot(in0 + in1, before, NN)
    take0 = jnp.where((in0 > 0.5) & (ahead == rank), 1.0, 0.0)
    take1 = jnp.where((in1 > 0.5) & (ahead + in0 == rank), 1.0, 0.0)

    to_scalar.wait()
    pltpu.make_async_copy(piece_in, piece_in, piece_recv).wait()

    def sort_part(d, _):
        part[d] = piece_in[bounded(ttab[0, d], PIECES)]
        return 0
    lax.fori_loop(0, N, sort_part, 0)

    crowd = jnp.sum(jnp.where(to1 == rows.astype(jnp.float32), 1.0, 0.0), axis=1, keepdims=True)
    worst = jnp.maximum(jnp.max(crowd, axis=0, keepdims=True), jnp.max(spares, axis=1, keepdims=True))
    facts0 = jnp.where(row8 == 0, by_source[1:2], jnp.where(row8 == 1, by_source[2:3], lanef))
    facts1 = jnp.where(row8 == 0, by_source[4:5], jnp.where(row8 == 1, by_source[5:6], jnp.where(row8 == 2, 1.0 * N, lanef + N)))
    facts = dot(facts0, take0, NT) + dot(facts1, take1, NT)

    own_part = pltpu.make_async_copy(part.at[me], part_in.at[me], part_recv)
    own_part.start()

    def pass_on(i, _):
        to = lax.rem(me + i, N)
        pltpu.make_async_remote_copy(
            src_ref=part.at[to], dst_ref=part_in.at[me], send_sem=part_send, recv_sem=part_recv,
            device_id=coords(to), device_id_type=MESH).start()
        return 0
    lax.fori_loop(1, N, pass_on, 0)

    lax.fori_loop(EARLY, N - lead, step, 0)

    def last(i, _):
        ship(i)
        return 0
    lax.fori_loop(N - lead, N, last, 0)

    same = jnp.where(rows // G == lanes // G, 1.0, 0.0)
    mean = dot(facts, same, NN) * (1.0 / G)
    centred = facts - mean
    spread = jnp.sqrt(dot(centred * centred, same, NN, exact=True) * (1.0 / G))
    adv = centred[0:1] / jnp.maximum(spread[0:1], 1.0)
    count = facts[1:2]
    weight = adv / count
    wrows = jnp.where(row8 == 0, weight, jnp.where((row8 == 1) & (count > 1.5), weight, 0.0))
    by0, by1 = dot(wrows, take0, NN, exact=True), dot(wrows, take1, NN, exact=True)
    mine1 = jnp.sum(by1 * here, axis=1, keepdims=True)
    wtab[0] = by0
    wtab[1] = mine1 + jnp.zeros((8, N), jnp.float32)
    to_scalar = pltpu.make_async_copy(wtab, wsm, tab_sem.at[1])
    to_scalar.start()
    weights_out[...] = by1
    table_out[...] = jnp.where(row8 == 0, facts[2:3], jnp.where(row8 == 1, facts[3:4], worst)).astype(jnp.int32)
    adv_out[...] = adv
    to_scalar.wait()
    fetch_gain.wait()
    gains = gbuf[...]

    def settle(i, _):
        src = await_row(i)
        outv[src] = scaled(recv[src], gains, wsm[0, 0, src], wsm[0, 1, src])
        return 0
    lax.fori_loop(0, LATE, settle, 0)

    pltpu.make_async_copy(part_in, part_in, part_recv).wait()

    def gather_part(t, _):
        extra_in[:, pl.ds(pl.multiple_of(t * 128, 128), 128)] = part_in[lax.rem(bounded(ttab[1, 0], N) + 4 * t, N)]
        return 0
    lax.fori_loop(0, PIECES, gather_part, 0)
    outv[N] = scaled(extra_in[...], gains, wsm[1, 0, 0], wsm[1, 1, 0])
    lax.fori_loop(LATE, N, settle, 0)
    put = pltpu.make_async_copy(outv, rows_out, out_sem)
    put.start()

    drained(meta, meta_send)
    tiles = piece_in.at[pl.ds(0, PIECES - 1)]
    pltpu.make_async_copy(tiles, tiles, piece_send).wait()
    drained(part, part_send)
    drained(send, send_sem)
    put.wait()


def second(hidden, gain, prompt_of, weights, rows_out, hbuf, gbuf, tab, itab, stab, send, recv, wsm, outv,
           in_sem, tab_sem, send_sem, recv_sem, out_sem):
    me = my_place()
    barrier = greet_all(me)
    copies = [pltpu.make_async_copy(a, b, in_sem.at[k]) for k, (a, b) in enumerate(
        ((hidden, hbuf), (gain, gbuf), (prompt_of, tab.at[pl.ds(0, 1)]), (weights, wsm)))]
    for copy in copies:
        copy.start()
    for copy in copies:
        copy.wait()
    rows = lax.broadcasted_iota(jnp.int32, (N, N), 0)
    lanes = lax.broadcasted_iota(jnp.int32, (N, N), 1)
    lanef = lax.broadcasted_iota(jnp.int32, (8, N), 1).astype(jnp.float32)
    slot1 = slots_of(tab[0:1] // OWN, rows, jnp.where(rows < lanes, 1.0, 0.0))[1]
    itab[...] = dot(lanef, slot1, NT).astype(jnp.int32)
    to_scalar = pltpu.make_async_copy(itab, stab, tab_sem)
    to_scalar.start()
    to_scalar.wait()
    pl.semaphore_wait(barrier, N - 1)
    pack, ship, await_row, own = row_traffic(me, hbuf, stab, send, recv, send_sem, recv_sem)

    def pack_all(i, _):
        pack(i)
        return 0
    lax.fori_loop(0, N, pack_all, 0)
    own.start()

    def ship_all(i, _):
        ship(i)
        return 0
    lax.fori_loop(1, N, ship_all, 0)
    gains = gbuf[...]

    def settle(i, _):
        src = await_row(i)
        outv[src] = scaled(recv[src], gains, wsm[0, src], wsm[1, src])
        return 0
    lax.fori_loop(0, N, settle, 0)
    put = pltpu.make_async_copy(outv, rows_out, out_sem)
    put.start()
    drained(send, send_sem)
    put.wait()


def arrange(table, adv_in, rows_in, out, adv_out, buf, in_sem, out_sem):
    CH = 16

    def load(q, _):
        pltpu.make_async_copy(rows_in.at[bounded(table[0, q], rows_in.shape[0])], buf.at[q], in_sem.at[q // CH]).start()
        return 0
    lax.fori_loop(0, N, load, 0)
    adv_out[...] = adv_in[...]
    for c in range(N // CH):
        part = pl.ds(c * CH, CH)
        pltpu.make_async_copy(buf.at[part], buf.at[part], in_sem.at[c]).wait()
        pltpu.make_async_copy(buf.at[part], out.at[part], out_sem).start()
    pltpu.make_async_copy(buf, buf, out_sem).wait()


def on_device(hidden, norm_gain, prompt_of, lengths, reward_level):
    count, window, features = hidden.shape
    bf16, f32, i32 = jnp.bfloat16, jnp.float32, jnp.int32
    shape = jax.ShapeDtypeStruct
    any_space = pl.BlockSpec(memory_space=pl.ANY)
    vmem = pl.BlockSpec(memory_space=pltpu.VMEM)
    dma = pltpu.SemaphoreType.DMA
    block = pltpu.VMEM((N, window, features), bf16)
    square, strip = pltpu.VMEM((N, N), i32), pltpu.VMEM((8, N), i32)
    gains = pltpu.VMEM((1, features), f32)
    gain, prompt, length, level = (a.reshape(1, a.shape[0]) for a in (norm_gain, prompt_of, lengths, reward_level))
    rows, table, adv, weights = pl.pallas_call(
        exchange,
        out_shape=(shape((N + 1, window, features), bf16), shape((8, N), i32), shape((1, N), f32), shape((8, N), f32)),
        in_specs=[any_space] * 5,
        out_specs=(any_space, vmem, vmem, vmem),
        scratch_shapes=[
            block, gains, strip, strip, pltpu.SMEM((8, N), i32), strip, pltpu.SMEM((8, N), i32), square, square,
            pltpu.VMEM((window, features), bf16), pltpu.VMEM((PIECES, window, 128), bf16),
            pltpu.VMEM((N, window, 128), bf16), pltpu.VMEM((N, window, 128), bf16), pltpu.VMEM((window, features), bf16),
            block, block, pltpu.VMEM((2, 8, N), f32), pltpu.SMEM((2, 8, N), f32),
            pltpu.VMEM((N + 1, window, features), bf16),
            dma((5,)), dma((2,)), dma, dma, dma, dma, dma, dma, dma, dma((N,)), dma],
        compiler_params=pltpu.CompilerParams(collective_id=0, has_side_effects=True),
        name="exchange",
    )(hidden, gain, prompt, length, level)

    def place(table, adv, rows):
        return pl.pallas_call(
            arrange,
            out_shape=(shape((N, window, features), bf16), shape((1, N), f32)),
            in_specs=[pl.BlockSpec(memory_space=pltpu.SMEM), vmem, any_space],
            out_specs=(any_space, vmem),
            scratch_shapes=[block, dma((8,)), dma],
            name="arrange",
        )(table, adv, rows)

    def few(args):
        return place(table, adv, rows)

    def many(args):
        more = pl.pallas_call(
            second,
            out_shape=shape((N, window, features), bf16),
            in_specs=[any_space] * 4,
            out_specs=any_space,
            scratch_shapes=[
                block, gains, strip, strip, pltpu.SMEM((8, N), i32), block, block, pltpu.SMEM((8, N), f32), block,
                dma((4,)), dma, dma, dma((N,)), dma],
            compiler_params=pltpu.CompilerParams(collective_id=1, has_side_effects=True),
            name="second",
        )(hidden, gain, prompt, weights)
        return place(table[1:2], adv, jnp.concatenate([rows[:N], more]))

    out, adv = lax.cond(table[2, 0] > 1, many, few, 0)
    return out, adv.reshape(N)


def solution(mesh):
    spec = P(AXES)
    return jax.shard_map(
        on_device, mesh=mesh, in_specs=(P(AXES, None, None), P(), spec, spec, spec),
        out_specs=(P(AXES, None, None), spec), check_vma=False)
```

```python
import functools

import jax
import jax.numpy as jnp
from jax import lax
from jax.experimental import pallas as pl
from jax.experimental.pallas import tpu as pltpu
from jax.sharding import PartitionSpec as P

LOGICAL = pl.DeviceIdType.LOGICAL
AXES = ("gx", "gy", "gz")
N = 128
G = 16
OWN = 8
PIECES = 32
EARLY = 48
LEAD = 4
BATCH = 8
LATE = 15
STRIDE = 37
norm_eps = 1e-05

NT = (((1,), (1,)), ((), ()))
NN = (((1,), (0,)), ((), ()))


def dot(a, b, dims, exact=False):
    if exact:
        return lax.dot_general(a, b, dims, precision=lax.Precision.HIGHEST,
                               preferred_element_type=jnp.float32)
    return lax.dot_general(a.astype(jnp.bfloat16), b.astype(jnp.bfloat16), dims,
                           preferred_element_type=jnp.float32)


class Place:
    def __init__(self):
        self.x, self.y, gz = lax.axis_index("gx"), lax.axis_index("gy"), lax.axis_index("gz")
        self.z, self.core = gz // 2, lax.rem(gz, 2)
        self.me = self.x * 32 + self.y * 8 + gz
        self.xs = [lax.rem(self.x + k, 4) * 32 for k in range(4)]
        self.ys = [lax.rem(self.y + k, 4) * 8 for k in range(4)]
        self.zs = [lax.rem(self.z + k, 4) * 2 for k in range(4)]
        self.cores = [lax.rem(self.core + k, 2) for k in range(2)]
        self.zc = [[z + c for c in self.cores] for z in self.zs]
        self.xy = [[a + b for b in self.ys] for a in self.xs]

    def target(self, i):
        o = (i * STRIDE) % N
        return self.xy[o // 32][o // 8 % 4] + self.zc[o // 2 % 4][o % 2]

    def target_of(self, i):
        o = lax.rem(i * STRIDE, N)
        return (lax.rem(self.x + o // 32, 4) * 32 + lax.rem(self.y + lax.rem(o // 8, 4), 4) * 8
                + lax.rem(self.z + lax.rem(o // 2, 4), 4) * 2 + lax.rem(self.core + lax.rem(o, 2), 2))

    def all(self, i, sign):
        o = (i * STRIDE) & (N - 1)
        return ((((self.x + sign * (o >> 5)) & 3) << 5) + (((self.y + sign * ((o >> 3) & 3)) & 3) << 3)
                + (((self.z + sign * ((o >> 1) & 3)) & 3) << 1) + ((self.core + o) & 1))

    def greet(self):
        barrier = pltpu.get_barrier_semaphore()
        for i in range(1, N):
            pl.semaphore_signal(barrier, inc=1, device_id=self.target(i), device_id_type=LOGICAL)
        return barrier


def ints(shape, dim):
    return lax.broadcasted_iota(jnp.int32, shape, dim)


def split(owner, target, ahead):
    mine = owner == target
    earlier = dot(jnp.where(mine, 1.0, 0.0), ahead, NN)
    return jnp.where(mine & (earlier < 0.5), 1.0, 0.0), jnp.where(mine & (earlier == 1.0), 1.0, 0.0)


def bounded(i, n):
    return jnp.clip(i, 0, n - 1)


def scaled(x, gains, w0, w1):
    token = ints((2, 1), 0)
    x = x.astype(jnp.float32)
    meansq = jnp.mean(x * x, axis=-1, keepdims=True)
    y = (x * lax.rsqrt(meansq + norm_eps) * gains).astype(jnp.bfloat16)
    return (y.astype(jnp.float32) * jnp.where(token == 0, w0, w1)).astype(jnp.bfloat16)


def whole(ref, sem):
    return pltpu.make_async_copy(ref, ref, sem)


def remote(src, dst, send_sem, recv_sem, to):
    return pltpu.make_async_remote_copy(src_ref=src, dst_ref=dst, send_sem=send_sem, recv_sem=recv_sem,
                                        device_id=to, device_id_type=LOGICAL)


def exchange(hidden, gain, prompt_of, lengths, reward, rows_out, table_out, flag_out, adv_out, weights_out,
             hbuf, gbuf, tab, itab, stab, jtab, ttab, meta, meta_in, extra, piece_in, part, part_in, extra_in,
             send, recv, wtab, wsm,
             in_sem, tab_sem, meta_send, meta_recv, piece_send, piece_recv, part_send, part_recv,
             send_sem, recv_sem):
    fetch_tab = [pltpu.make_async_copy(ref, tab.at[pl.ds(k, 1)], in_sem.at[2 + k])
                 for k, ref in enumerate((prompt_of, lengths, reward))]
    fetch_rows = pltpu.make_async_copy(hidden, hbuf, in_sem.at[0])
    fetch_gain = pltpu.make_async_copy(gain, gbuf, in_sem.at[1])
    for copy in fetch_tab:
        copy.start()
    fetch_rows.start()
    fetch_gain.start()
    place = Place()
    me = place.me
    barrier = place.greet()
    for copy in fetch_tab:
        copy.wait()

    rows, lanes = ints((N, N), 0), ints((N, N), 1)
    row8, lane8 = ints((8, N), 0), ints((8, N), 1)
    lane1 = ints((1, N), 1)
    lanef = lane8.astype(jnp.float32)
    target = place.all(rows, 1)

    prompt, length, level = tab[0:1], tab[1:2], tab[2:3]
    owner, label = prompt // OWN, lax.rem(prompt, OWN) + 1
    slot0, slot1 = split(owner, target, jnp.where(rows < lanes, 1.0, 0.0))
    twice = jnp.sum(slot1, axis=0, keepdims=True)
    spare = jnp.sum(twice, axis=1, keepdims=True)
    spare_row = jnp.sum(twice * lane1.astype(jnp.float32), axis=1, keepdims=True)
    spare_to = jnp.where(spare > 0.5, jnp.sum(twice * owner.astype(jnp.float32), axis=1, keepdims=True), -1.0)
    itab[...] = jnp.where(row8 == 0, dot(lanef, slot0, NT), spare_row).astype(jnp.int32)
    to_scalar = pltpu.make_async_copy(itab, stab, tab_sem.at[0])
    to_scalar.start()
    zero = jnp.zeros((N, N), jnp.int32)
    told = jnp.where(rows == 0, label, jnp.where(rows == 1, level, jnp.where(rows == 2, length, zero)))
    told1 = jnp.where(rows == 3, label, jnp.where(rows == 4, level, jnp.where(rows == 5, length, zero)))
    meta[...] = (dot(slot0, told.astype(jnp.float32), NT) + dot(slot1, told1.astype(jnp.float32), NT)
                 + jnp.where(lanes == 6, spare_to, jnp.where(lanes == 7, spare, 0.0))).astype(jnp.int32)
    to_scalar.wait()
    fetch_rows.wait()
    extra[...] = hbuf[bounded(stab[1, 0], N)]

    def pack(i):
        send[i] = hbuf[bounded(stab[0, i], N)]

    def ship(i):
        remote(send.at[i], recv.at[i], send_sem, recv_sem.at[i // BATCH], place.target(i)).start()

    for i in range(LEAD + 1):
        pack(i)
    own = pltpu.make_async_copy(send.at[0], recv.at[0], recv_sem.at[0])
    own_meta = pltpu.make_async_copy(meta.at[pl.ds(0, 1)], meta_in.at[pl.ds(0, 1)], meta_recv)
    own_piece = pltpu.make_async_copy(extra.at[:, pl.ds(0, 128)], piece_in.at[me // 4], piece_recv)
    own.start()
    own_meta.start()
    own_piece.start()

    pl.semaphore_wait(barrier, N - 1)

    for i in range(1, N):
        remote(meta.at[pl.ds(i, 1)], meta_in.at[pl.ds(i, 1)], meta_send, meta_recv, place.target(i)).start()
    for t in range(1, PIECES):
        remote(extra.at[:, pl.ds(t * 128, 128)], piece_in.at[me // 4], piece_send, piece_recv,
               lax.rem(me + 4 * t, N)).start()
    for i in range(1, EARLY):
        pack(i + LEAD)
        ship(i)

    whole(meta_in, meta_recv).wait()
    told_in = meta_in[...].astype(jnp.float32)
    by_step = dot(jnp.where(row8 == lane8, 1.0, 0.0), told_in, NT)
    label0, label1, to1, spares = by_step[0:1], by_step[3:4], by_step[6:7], by_step[7:8]
    source = place.all(lane1, -1)

    goes = to1 == target.astype(jnp.float32)
    passing = jnp.where(goes & (lax.rem(source, 4) == lax.rem(me, 4)), 1.0, 0.0)
    piece_of = dot((place.all(lane8, -1) // 4).astype(jnp.float32), passing, NT)
    here = jnp.where(to1 == me.astype(jnp.float32), 1.0, 0.0)
    giver = jnp.sum(here * source.astype(jnp.float32), axis=1, keepdims=True)
    jtab[...] = jnp.where(row8 == 0, piece_of, giver).astype(jnp.int32)
    to_scalar = pltpu.make_async_copy(jtab, ttab, tab_sem.at[0])
    to_scalar.start()

    ahead = jnp.where(place.all(rows, -1) < source, 1.0, 0.0)
    group = (rows // G + 1).astype(jnp.float32)
    rank = lax.rem(rows, G).astype(jnp.float32)
    in0, in1 = jnp.where(label0 == group, 1.0, 0.0), jnp.where(label1 == group, 1.0, 0.0)
    passed = dot(in0 + in1, ahead, NN)
    take0 = jnp.where((in0 > 0.5) & (passed == rank), 1.0, 0.0)
    take1 = jnp.where((in1 > 0.5) & (passed + in0 == rank), 1.0, 0.0)

    to_scalar.wait()
    whole(piece_in, piece_recv).wait()
    for i in range(N):
        part[i] = piece_in[bounded(ttab[0, i], PIECES)]

    crowd = jnp.sum(jnp.where(goes, 1.0, 0.0), axis=1, keepdims=True)
    worst = jnp.maximum(jnp.max(crowd, axis=0, keepdims=True), jnp.max(spares, axis=1, keepdims=True))
    facts0 = jnp.where(row8 == 0, by_step[1:2], jnp.where(row8 == 1, by_step[2:3], lanef))
    facts1 = jnp.where(row8 == 0, by_step[4:5], jnp.where(row8 == 1, by_step[5:6], jnp.where(row8 == 2, 1.0 * N, lanef + N)))
    facts = dot(facts0, take0, NT) + dot(facts1, take1, NT)

    own_part = pltpu.make_async_copy(part.at[0], part_in.at[me], part_recv)
    own_part.start()
    for i in range(1, N):
        remote(part.at[i], part_in.at[me], part_send, part_recv, place.target(i)).start()
    for i in range(EARLY, N):
        if i + LEAD < N:
            pack(i + LEAD)
        ship(i)

    same = jnp.where(rows // G == lanes // G, 1.0, 0.0)
    mean = dot(facts, same, NN) * (1.0 / G)
    centred = facts - mean
    spread = jnp.sqrt(dot(centred * centred, same, NN, exact=True) * (1.0 / G))
    adv = centred[0:1] / jnp.maximum(spread[0:1], 1.0)
    count = facts[1:2]
    weight = adv / count
    wrows = jnp.where(row8 == 0, weight, jnp.where((row8 == 1) & (count > 1.5), weight, 0.0))
    by0, by1 = dot(wrows, take0, NN, exact=True), dot(wrows, take1, NN, exact=True)
    wtab[0] = by0
    wtab[1] = jnp.sum(by1 * here, axis=1, keepdims=True) + jnp.zeros((8, N), jnp.float32)
    to_scalar = pltpu.make_async_copy(wtab, wsm, tab_sem.at[1])
    to_scalar.start()
    weights_out[...] = by1
    table_out[...] = jnp.where(row8 == 0, facts[2:3], facts[3:4]).astype(jnp.int32)
    flag_out[...] = worst.astype(jnp.int32)
    adv_out[...] = adv
    to_scalar.wait()
    fetch_gain.wait()
    gains = gbuf[...]

    def settle(g, _):
        whole(recv.at[pl.ds(0, BATCH)], recv_sem.at[g]).wait()
        for k in range(BATCH):
            i = g * BATCH + k
            rows_out[i] = scaled(recv[i], gains, wsm[0, 0, i], wsm[0, 1, i])
        return 0
    lax.fori_loop(0, LATE, settle, 0)

    whole(part_in, part_recv).wait()
    giver = bounded(ttab[1, 0], N)
    for t in range(PIECES):
        extra_in[:, pl.ds(t * 128, 128)] = part_in[lax.rem(giver + 4 * t, N)]
    rows_out[N] = scaled(extra_in[...], gains, wsm[1, 0, 0], wsm[1, 1, 0])
    lax.fori_loop(LATE, N // BATCH, settle, 0)

    whole(meta.at[pl.ds(0, N - 1)], meta_send).wait()
    whole(piece_in.at[pl.ds(0, PIECES - 1)], piece_send).wait()
    whole(part.at[pl.ds(0, N - 1)], part_send).wait()
    whole(send.at[pl.ds(0, N - 1)], send_sem).wait()


def second(hidden, gain, prompt_of, weights, rows_out, hbuf, gbuf, tab, itab, stab, send, recv, wsm, outv,
           in_sem, tab_sem, send_sem, recv_sem, out_sem):
    copies = [pltpu.make_async_copy(a, b, in_sem.at[k]) for k, (a, b) in enumerate(
        ((hidden, hbuf), (gain, gbuf), (prompt_of, tab.at[pl.ds(0, 1)]), (weights, wsm)))]
    for copy in copies:
        copy.start()
    place = Place()
    barrier = place.greet()
    for copy in copies:
        copy.wait()
    rows, lanes = ints((N, N), 0), ints((N, N), 1)
    slot1 = split(tab[0:1] // OWN, place.all(rows, 1), jnp.where(rows < lanes, 1.0, 0.0))[1]
    itab[...] = dot(ints((8, N), 1).astype(jnp.float32), slot1, NT).astype(jnp.int32)
    to_scalar = pltpu.make_async_copy(itab, stab, tab_sem)
    to_scalar.start()
    to_scalar.wait()
    pl.semaphore_wait(barrier, N - 1)

    def pack(i, _):
        send[i] = hbuf[bounded(stab[0, i], N)]
        return 0
    lax.fori_loop(0, N, pack, 0)
    pltpu.make_async_copy(send.at[0], recv.at[0], recv_sem).start()

    def ship(i, _):
        remote(send.at[i], recv.at[i], send_sem, recv_sem, place.target_of(i)).start()
        return 0
    lax.fori_loop(1, N, ship, 0)
    whole(recv, recv_sem).wait()
    gains = gbuf[...]

    def settle(i, _):
        outv[i] = scaled(recv[i], gains, wsm[0, i], wsm[1, i])
        return 0
    lax.fori_loop(0, N, settle, 0)
    whole(send.at[pl.ds(0, N - 1)], send_sem).wait()
    put = pltpu.make_async_copy(outv, rows_out, out_sem)
    put.start()
    put.wait()


def arrange(table, adv_in, rows_in, out, adv_out, sem):
    for q in range(N):
        pltpu.make_async_copy(rows_in.at[bounded(table[0, q], rows_in.shape[0])], out.at[q], sem).start()
    adv_out[...] = adv_in[...]
    whole(out, sem).wait()


def on_device(hidden, norm_gain, prompt_of, lengths, reward_level):
    count, window, features = hidden.shape
    bf16, f32, i32 = jnp.bfloat16, jnp.float32, jnp.int32
    shape = jax.ShapeDtypeStruct
    any_space = pl.BlockSpec(memory_space=pl.ANY)
    vmem = pl.BlockSpec(memory_space=pltpu.VMEM)
    dma = pltpu.SemaphoreType.DMA
    block = pltpu.VMEM((N, window, features), bf16)
    square, strip = pltpu.VMEM((N, N), i32), pltpu.VMEM((8, N), i32)
    gains = pltpu.VMEM((1, features), f32)
    gain, prompt, length, level = (a.reshape(1, a.shape[0]) for a in (norm_gain, prompt_of, lengths, reward_level))
    rows, table, flag, adv, weights = pl.pallas_call(
        exchange,
        out_shape=(shape((N + 1, window, features), bf16), shape((8, N), i32), shape((1, 1), i32),
                   shape((1, N), f32), shape((8, N), f32)),
        in_specs=[any_space] * 5,
        out_specs=(vmem,) * 5,
        scratch_shapes=[
            block, gains, strip, strip, pltpu.SMEM((8, N), i32), strip, pltpu.SMEM((8, N), i32), square, square,
            pltpu.VMEM((window, features), bf16), pltpu.VMEM((PIECES, window, 128), bf16),
            pltpu.VMEM((N, window, 128), bf16), pltpu.VMEM((N, window, 128), bf16), pltpu.VMEM((window, features), bf16),
            block, block, pltpu.VMEM((2, 8, N), f32), pltpu.SMEM((2, 8, N), f32),
            dma((5,)), dma((2,)), dma, dma, dma, dma, dma, dma, dma, dma((N // BATCH,))],
        compiler_params=pltpu.CompilerParams(collective_id=0, has_side_effects=True),
        name="exchange",
    )(hidden, gain, prompt, length, level)

    def put(table, adv, rows):
        return pl.pallas_call(
            arrange,
            out_shape=(shape((N, window, features), bf16), shape((1, N), f32)),
            in_specs=[pl.BlockSpec(memory_space=pltpu.SMEM), vmem, any_space],
            out_specs=(any_space, vmem),
            scratch_shapes=[dma],
            name="arrange",
        )(table, adv, rows)

    def few(_):
        return put(table, adv, rows)

    def many(_):
        more = pl.pallas_call(
            second,
            out_shape=shape((N, window, features), bf16),
            in_specs=[any_space] * 4,
            out_specs=any_space,
            scratch_shapes=[
                block, gains, strip, strip, pltpu.SMEM((8, N), i32), block, block, pltpu.SMEM((8, N), f32), block,
                dma((4,)), dma, dma, dma, dma],
            compiler_params=pltpu.CompilerParams(collective_id=1, has_side_effects=True),
            name="second",
        )(hidden, gain, prompt, weights)
        return put(table[1:2], adv, jnp.concatenate([rows[:N], more]))

    out, adv = lax.cond(flag[0, 0] > 1, many, few, 0)
    return out, adv.reshape(N)


def solution(mesh):
    spec = P(AXES)
    return jax.shard_map(
        on_device, mesh=mesh, in_specs=(P(AXES, None, None), P(), spec, spec, spec),
        out_specs=(P(AXES, None, None), spec), check_vma=False)
```

```python
import functools

import jax
import jax.numpy as jnp
from jax import lax
from jax.experimental import pallas as pl
from jax.experimental.pallas import tpu as pltpu
from jax.sharding import PartitionSpec as P

LOGICAL = pl.DeviceIdType.LOGICAL
AXES = ("gx", "gy", "gz")
N = 128
G = 16
OWN = 8
PIECES = 32
EARLY = 48
LEAD = 4
FIRST = 8
READY = 16
BATCH = 8
LATE = 15
STRIDE = 37
norm_eps = 1e-05

NT = (((1,), (1,)), ((), ()))
NN = (((1,), (0,)), ((), ()))


def dot(a, b, dims, exact=False):
    if exact:
        return lax.dot_general(a, b, dims, precision=lax.Precision.HIGHEST,
                               preferred_element_type=jnp.float32)
    return lax.dot_general(a.astype(jnp.bfloat16), b.astype(jnp.bfloat16), dims,
                           preferred_element_type=jnp.float32)


def hops(i):
    o = (i * STRIDE) % N
    return sum(min(k, 4 - k) for k in (o // 32, o // 8 % 4, o // 2 % 4))


class Place:
    def __init__(self):
        self.x, self.y, gz = lax.axis_index("gx"), lax.axis_index("gy"), lax.axis_index("gz")
        self.z, self.core = gz // 2, lax.rem(gz, 2)
        self.me = self.x * 32 + self.y * 8 + gz
        self.xs = [lax.rem(self.x + k, 4) * 32 for k in range(4)]
        self.ys = [lax.rem(self.y + k, 4) * 8 for k in range(4)]
        self.zs = [lax.rem(self.z + k, 4) * 2 for k in range(4)]
        self.cores = [lax.rem(self.core + k, 2) for k in range(2)]
        self.zc = [[z + c for c in self.cores] for z in self.zs]
        self.xy = [[a + b for b in self.ys] for a in self.xs]

    def target(self, i):
        o = (i * STRIDE) % N
        return self.xy[o // 32][o // 8 % 4] + self.zc[o // 2 % 4][o % 2]

    def target_of(self, i):
        o = lax.rem(i * STRIDE, N)
        return (lax.rem(self.x + o // 32, 4) * 32 + lax.rem(self.y + lax.rem(o // 8, 4), 4) * 8
                + lax.rem(self.z + lax.rem(o // 2, 4), 4) * 2 + lax.rem(self.core + lax.rem(o, 2), 2))

    def all(self, i, sign):
        o = (i * STRIDE) & (N - 1)
        return ((((self.x + sign * (o >> 5)) & 3) << 5) + (((self.y + sign * ((o >> 3) & 3)) & 3) << 3)
                + (((self.z + sign * ((o >> 1) & 3)) & 3) << 1) + ((self.core + o) & 1))

    def greet(self):
        barrier = pltpu.get_barrier_semaphore()
        for i in sorted(range(1, N), key=hops, reverse=True):
            pl.semaphore_signal(barrier, inc=1, device_id=self.target(i), device_id_type=LOGICAL)
        return barrier


def ints(shape, dim):
    return lax.broadcasted_iota(jnp.int32, shape, dim)


def split(owner, target, ahead):
    mine = owner == target
    earlier = dot(jnp.where(mine, 1.0, 0.0), ahead, NN)
    return jnp.where(mine & (earlier < 0.5), 1.0, 0.0), jnp.where(mine & (earlier == 1.0), 1.0, 0.0)


def bounded(i, n):
    return jnp.clip(i, 0, n - 1)


def normed(x, gains):
    x = x.astype(jnp.float32)
    meansq = jnp.mean(x * x, axis=-1, keepdims=True)
    return (x * lax.rsqrt(meansq + norm_eps) * gains).astype(jnp.bfloat16)


def weighed(y, w0, w1):
    return (y.astype(jnp.float32) * jnp.where(ints((2, 1), 0) == 0, w0, w1)).astype(jnp.bfloat16)


def whole(ref, sem):
    return pltpu.make_async_copy(ref, ref, sem)


def remote(src, dst, send_sem, recv_sem, to):
    return pltpu.make_async_remote_copy(src_ref=src, dst_ref=dst, send_sem=send_sem, recv_sem=recv_sem,
                                        device_id=to, device_id_type=LOGICAL)


def exchange(hidden, gain, prompt_of, lengths, reward, rows_out, table_out, flag_out, adv_out, weights_out,
             hbuf, gbuf, tab, itab, stab, jtab, ttab, meta, meta_in, extra, piece_in, part, part_in, extra_in,
             send, recv, wtab, wsm, flag,
             in_sem, tab_sem, meta_send, meta_recv, piece_send, piece_recv, part_send, part_recv,
             send_sem, recv_sem):
    fetch_tab = [pltpu.make_async_copy(ref, tab.at[pl.ds(k, 1)], in_sem.at[2 + k])
                 for k, ref in enumerate((prompt_of, lengths, reward))]
    fetch_rows = pltpu.make_async_copy(hidden, hbuf, in_sem.at[0])
    fetch_gain = pltpu.make_async_copy(gain, gbuf, in_sem.at[1])
    for copy in fetch_tab:
        copy.start()
    fetch_rows.start()
    fetch_gain.start()
    place = Place()
    me = place.me
    barrier = place.greet()
    for copy in fetch_tab:
        copy.wait()

    rows, lanes = ints((N, N), 0), ints((N, N), 1)
    row8, lane8 = ints((8, N), 0), ints((8, N), 1)
    lane1 = ints((1, N), 1)
    lanef = lane8.astype(jnp.float32)
    target = place.all(rows, 1)

    prompt, length, level = tab[0:1], tab[1:2], tab[2:3]
    owner, label = prompt // OWN, lax.rem(prompt, OWN) + 1
    slot0, slot1 = split(owner, target, jnp.where(rows < lanes, 1.0, 0.0))
    twice = jnp.sum(slot1, axis=0, keepdims=True)
    spare = jnp.sum(twice, axis=1, keepdims=True)
    spare_row = jnp.sum(twice * lane1.astype(jnp.float32), axis=1, keepdims=True)
    spare_to = jnp.where(spare > 0.5, jnp.sum(twice * owner.astype(jnp.float32), axis=1, keepdims=True), -1.0)
    itab[...] = jnp.where(row8 == 0, dot(lanef, slot0, NT), spare_row).astype(jnp.int32)
    to_scalar = pltpu.make_async_copy(itab, stab, tab_sem.at[0])
    to_scalar.start()
    zero = jnp.zeros((N, N), jnp.int32)
    told = jnp.where(rows == 0, label, jnp.where(rows == 1, level, jnp.where(rows == 2, length, zero)))
    told1 = jnp.where(rows == 3, label, jnp.where(rows == 4, level, jnp.where(rows == 5, length, zero)))
    meta[...] = (dot(slot0, told.astype(jnp.float32), NT) + dot(slot1, told1.astype(jnp.float32), NT)
                 + jnp.where(lanes == 6, spare_to, jnp.where(lanes == 7, spare, 0.0))).astype(jnp.int32)
    to_scalar.wait()
    fetch_gain.wait()
    gains = gbuf[...]
    fetch_rows.wait()
    extra[...] = normed(hbuf[bounded(stab[1, 0], N)], gains)

    def pack(i):
        if i < N:
            send[i] = normed(hbuf[bounded(stab[0, i], N)], gains)

    def ship(i):
        remote(send.at[i], recv.at[i], send_sem, recv_sem.at[i // BATCH], place.target(i)).start()

    def hand(r):
        t = lax.rem(me // 4 + r, PIECES)
        return extra.at[:, pl.ds(pl.multiple_of(t * 128, 128), 128)], 4 * t

    relay = lax.rem(me, 4) == 0
    for i in range(READY):
        pack(i)
    pltpu.make_async_copy(send.at[0], recv.at[0], recv_sem.at[0]).start()
    pltpu.make_async_copy(meta.at[pl.ds(0, 1)], meta_in.at[pl.ds(0, 1)], meta_recv).start()

    @pl.when(relay)
    def _():
        pltpu.make_async_copy(hand(0)[0], piece_in.at[me], piece_recv).start()

    pl.semaphore_wait(barrier, N - 1)

    for i in range(1, FIRST):
        ship(i)
    for i in range(1, N):
        remote(meta.at[pl.ds(i, 1)], meta_in.at[pl.ds(i, 1)], meta_send, meta_recv, place.target(i)).start()

    @pl.when(jnp.logical_not(relay))
    def _():
        tile, to = hand(0)
        remote(tile, piece_in.at[me], piece_send, piece_recv, to).start()
    for r in range(1, PIECES):
        tile, to = hand(r)
        remote(tile, piece_in.at[me], piece_send, piece_recv, to).start()
    for i in range(FIRST, EARLY):
        pack(i - FIRST + READY)
        ship(i)

    whole(meta_in, meta_recv).wait()
    told_in = meta_in[...].astype(jnp.float32)
    by_step = dot(jnp.where(row8 == lane8, 1.0, 0.0), told_in, NT)
    label0, label1, to1, spares = by_step[0:1], by_step[3:4], by_step[6:7], by_step[7:8]
    source = place.all(lane1, -1)

    goes = to1 == target.astype(jnp.float32)
    jtab[...] = dot(place.all(lane8, -1).astype(jnp.float32), jnp.where(goes, 1.0, 0.0), NT).astype(jnp.int32)
    to_scalar = pltpu.make_async_copy(jtab, ttab, tab_sem.at[0])
    to_scalar.start()
    here = jnp.where(to1 == me.astype(jnp.float32), 1.0, 0.0)

    ahead = jnp.where(place.all(rows, -1) < source, 1.0, 0.0)
    group = (rows // G + 1).astype(jnp.float32)
    rank = lax.rem(rows, G).astype(jnp.float32)
    in0, in1 = jnp.where(label0 == group, 1.0, 0.0), jnp.where(label1 == group, 1.0, 0.0)
    passed = dot(in0 + in1, ahead, NN)
    take0 = jnp.where((in0 > 0.5) & (passed == rank), 1.0, 0.0)
    take1 = jnp.where((in1 > 0.5) & (passed + in0 == rank), 1.0, 0.0)

    crowd = jnp.sum(jnp.where(goes, 1.0, 0.0), axis=1, keepdims=True)
    worst = jnp.maximum(jnp.max(crowd, axis=0, keepdims=True), jnp.max(spares, axis=1, keepdims=True))
    facts0 = jnp.where(row8 == 0, by_step[1:2], jnp.where(row8 == 1, by_step[2:3], lanef))
    facts1 = jnp.where(row8 == 0, by_step[4:5], jnp.where(row8 == 1, by_step[5:6], jnp.where(row8 == 2, 1.0 * N, lanef + N)))
    facts = dot(facts0, take0, NT) + dot(facts1, take1, NT)

    flag[...] = worst.astype(jnp.int32)
    flag_copy = pltpu.make_async_copy(flag, flag_out, in_sem.at[0])
    flag_copy.start()
    to_scalar.wait()

    @pl.when(relay)
    def _():
        whole(piece_in, piece_recv).wait()
        for i in range(N):
            part[i] = piece_in[bounded(ttab[0, i], N)]
        for i in range(EARLY, EARLY + LEAD):
            ship(i)
        pltpu.make_async_copy(part.at[0], part_in.at[me // 4], part_recv).start()
        for i in range(1, N):
            remote(part.at[i], part_in.at[me // 4], part_send, part_recv, place.target(i)).start()

    @pl.when(jnp.logical_not(relay))
    def _():
        for i in range(EARLY, EARLY + LEAD):
            ship(i)
    for i in range(EARLY + LEAD, N):
        pack(i - FIRST - LEAD + READY)
        ship(i)

    same = jnp.where(rows // G == lanes // G, 1.0, 0.0)
    mean = dot(facts, same, NN) * (1.0 / G)
    centred = facts - mean
    spread = jnp.sqrt(dot(centred * centred, same, NN, exact=True) * (1.0 / G))
    adv = centred[0:1] / jnp.maximum(spread[0:1], 1.0)
    count = facts[1:2]
    weight = adv / count
    wrows = jnp.where(row8 == 0, weight, jnp.where((row8 == 1) & (count > 1.5), weight, 0.0))
    by0, by1 = dot(wrows, take0, NN, exact=True), dot(wrows, take1, NN, exact=True)
    wtab[0] = by0
    wtab[1] = jnp.sum(by1 * here, axis=1, keepdims=True) + jnp.zeros((8, N), jnp.float32)
    to_scalar = pltpu.make_async_copy(wtab, wsm, tab_sem.at[1])
    to_scalar.start()
    weights_out[...] = by1
    table_out[...] = jnp.where(row8 == 0, facts[2:3], facts[3:4]).astype(jnp.int32)
    adv_out[...] = adv
    to_scalar.wait()

    def settle(g, _):
        whole(recv.at[pl.ds(0, BATCH)], recv_sem.at[g]).wait()
        for k in range(BATCH):
            i = g * BATCH + k
            rows_out[i] = weighed(recv[i], wsm[0, 0, i], wsm[0, 1, i])
        return 0
    lax.fori_loop(0, LATE, settle, 0)

    whole(part_in, part_recv).wait()
    for t in range(PIECES):
        extra_in[:, pl.ds(t * 128, 128)] = part_in[t]
    rows_out[N] = weighed(extra_in[...], wsm[1, 0, 0], wsm[1, 1, 0])
    lax.fori_loop(LATE, N // BATCH, settle, 0)

    whole(meta.at[pl.ds(0, N - 1)], meta_send).wait()
    whole(send.at[pl.ds(0, N - 1)], send_sem).wait()
    flag_copy.wait()

    @pl.when(relay)
    def _():
        whole(piece_in.at[pl.ds(0, PIECES - 1)], piece_send).wait()
        whole(part.at[pl.ds(0, N - 1)], part_send).wait()

    @pl.when(jnp.logical_not(relay))
    def _():
        whole(piece_in.at[pl.ds(0, PIECES)], piece_send).wait()


def second(hidden, gain, prompt_of, weights, rows_out, hbuf, gbuf, tab, itab, stab, send, recv, wsm, outv,
           in_sem, tab_sem, send_sem, recv_sem, out_sem):
    copies = [pltpu.make_async_copy(a, b, in_sem.at[k]) for k, (a, b) in enumerate(
        ((hidden, hbuf), (gain, gbuf), (prompt_of, tab.at[pl.ds(0, 1)]), (weights, wsm)))]
    for copy in copies:
        copy.start()
    place = Place()
    barrier = place.greet()
    for copy in copies:
        copy.wait()
    rows, lanes = ints((N, N), 0), ints((N, N), 1)
    slot1 = split(tab[0:1] // OWN, place.all(rows, 1), jnp.where(rows < lanes, 1.0, 0.0))[1]
    itab[...] = dot(ints((8, N), 1).astype(jnp.float32), slot1, NT).astype(jnp.int32)
    to_scalar = pltpu.make_async_copy(itab, stab, tab_sem)
    to_scalar.start()
    to_scalar.wait()
    pl.semaphore_wait(barrier, N - 1)

    def pack(i, _):
        send[i] = hbuf[bounded(stab[0, i], N)]
        return 0
    lax.fori_loop(0, N, pack, 0)
    pltpu.make_async_copy(send.at[0], recv.at[0], recv_sem).start()

    def ship(i, _):
        remote(send.at[i], recv.at[i], send_sem, recv_sem, place.target_of(i)).start()
        return 0
    lax.fori_loop(1, N, ship, 0)
    whole(recv, recv_sem).wait()
    gains = gbuf[...]

    def settle(i, _):
        outv[i] = weighed(normed(recv[i], gains), wsm[0, i], wsm[1, i])
        return 0
    lax.fori_loop(0, N, settle, 0)
    whole(send.at[pl.ds(0, N - 1)], send_sem).wait()
    put = pltpu.make_async_copy(outv, rows_out, out_sem)
    put.start()
    put.wait()


def arrange(table, adv_in, rows_in, out, adv_out, sem):
    for q in range(N):
        pltpu.make_async_copy(rows_in.at[bounded(table[0, q], rows_in.shape[0])], out.at[q], sem).start()
    adv_out[...] = adv_in[...]
    whole(out, sem).wait()


def on_device(hidden, norm_gain, prompt_of, lengths, reward_level):
    count, window, features = hidden.shape
    bf16, f32, i32 = jnp.bfloat16, jnp.float32, jnp.int32
    shape = jax.ShapeDtypeStruct
    any_space = pl.BlockSpec(memory_space=pl.ANY)
    vmem = pl.BlockSpec(memory_space=pltpu.VMEM)
    dma = pltpu.SemaphoreType.DMA
    block = pltpu.VMEM((N, window, features), bf16)
    square, strip = pltpu.VMEM((N, N), i32), pltpu.VMEM((8, N), i32)
    gains = pltpu.VMEM((1, features), f32)
    gain, prompt, length, level = (a.reshape(1, a.shape[0]) for a in (norm_gain, prompt_of, lengths, reward_level))
    rows, table, flag, adv, weights = pl.pallas_call(
        exchange,
        out_shape=(shape((N + 1, window, features), bf16), shape((8, N), i32), shape((1, 1), i32),
                   shape((1, N), f32), shape((8, N), f32)),
        in_specs=[any_space] * 5,
        out_specs=(vmem, vmem, any_space, vmem, vmem),
        scratch_shapes=[
            block, gains, strip, strip, pltpu.SMEM((8, N), i32), strip, pltpu.SMEM((8, N), i32), square, square,
            pltpu.VMEM((window, features), bf16), pltpu.VMEM((N, window, 128), bf16),
            pltpu.VMEM((N, window, 128), bf16), pltpu.VMEM((PIECES, window, 128), bf16), pltpu.VMEM((window, features), bf16),
            block, block, pltpu.VMEM((2, 8, N), f32), pltpu.SMEM((2, 8, N), f32), pltpu.VMEM((1, 1), i32),
            dma((5,)), dma((2,)), dma, dma, dma, dma, dma, dma, dma, dma((N // BATCH,))],
        compiler_params=pltpu.CompilerParams(collective_id=0, has_side_effects=True),
        name="exchange",
    )(hidden, gain, prompt, length, level)

    def put(table, adv, rows):
        return pl.pallas_call(
            arrange,
            out_shape=(shape((N, window, features), bf16), shape((1, N), f32)),
            in_specs=[pl.BlockSpec(memory_space=pltpu.SMEM), vmem, any_space],
            out_specs=(any_space, vmem),
            scratch_shapes=[dma],
            name="arrange",
        )(table, adv, rows)

    def few(_):
        return put(table, adv, rows)

    def many(_):
        more = pl.pallas_call(
            second,
            out_shape=shape((N, window, features), bf16),
            in_specs=[any_space] * 4,
            out_specs=any_space,
            scratch_shapes=[
                block, gains, strip, strip, pltpu.SMEM((8, N), i32), block, block, pltpu.SMEM((8, N), f32), block,
                dma((4,)), dma, dma, dma, dma],
            compiler_params=pltpu.CompilerParams(collective_id=1, has_side_effects=True),
            name="second",
        )(hidden, gain, prompt, weights)
        return put(table[1:2], adv, jnp.concatenate([rows[:N], more]))

    out, adv = lax.cond(flag[0, 0] > 1, many, few, 0)
    return out, adv.reshape(N)


def solution(mesh):
    spec = P(AXES)
    return jax.shard_map(
        on_device, mesh=mesh, in_specs=(P(AXES, None, None), P(), spec, spec, spec),
        out_specs=(P(AXES, None, None), spec), check_vma=False)
```

```python
import random

import jax
import jax.numpy as jnp
import numpy as np
from jax import lax
from jax.experimental import pallas as pl
from jax.experimental.pallas import tpu as pltpu
from jax.sharding import PartitionSpec as P

LOGICAL = pl.DeviceIdType.LOGICAL
AXES = ("gx", "gy", "gz")
N = 128
G = 16
OWN = 8
PIECES = 32
EARLY = 48
LEAD = 4
FIRST = 8
READY = 16
BATCH = 8
LATE = 15
SEED = 0
norm_eps = 1e-05

NT = (((1,), (1,)), ((), ()))
NN = (((1,), (0,)), ((), ()))


def hops(o):
    return sum(min(k, 4 - k) for k in (o // 32, o // 8 % 4, o // 2 % 4))


def make_order(seed):
    rest = list(range(1, N))
    random.Random(seed).shuffle(rest)
    return [0] + sorted(rest, key=lambda o: hops(o) < 3)


ORDER = make_order(SEED)


def dot(a, b, dims, exact=False):
    if exact:
        return lax.dot_general(a, b, dims, precision=lax.Precision.HIGHEST,
                               preferred_element_type=jnp.float32)
    return lax.dot_general(a.astype(jnp.bfloat16), b.astype(jnp.bfloat16), dims,
                           preferred_element_type=jnp.float32)


class Place:
    def __init__(self):
        self.x, self.y, gz = lax.axis_index("gx"), lax.axis_index("gy"), lax.axis_index("gz")
        self.z, self.core = gz // 2, lax.rem(gz, 2)
        self.me = self.x * 32 + self.y * 8 + gz
        self.xs = [lax.rem(self.x + k, 4) * 32 for k in range(4)]
        self.ys = [lax.rem(self.y + k, 4) * 8 for k in range(4)]
        self.zs = [lax.rem(self.z + k, 4) * 2 for k in range(4)]
        self.cores = [lax.rem(self.core + k, 2) for k in range(2)]
        self.zc = [[z + c for c in self.cores] for z in self.zs]
        self.xy = [[a + b for b in self.ys] for a in self.xs]

    def target(self, i):
        o = ORDER[i]
        return self.xy[o // 32][o // 8 % 4] + self.zc[o // 2 % 4][o % 2]

    def all(self, o, sign):
        return ((((self.x + sign * (o >> 5)) & 3) << 5) + (((self.y + sign * ((o >> 3) & 3)) & 3) << 3)
                + (((self.z + sign * ((o >> 1) & 3)) & 3) << 1) + ((self.core + o) & 1))

    def greet(self):
        barrier = pltpu.get_barrier_semaphore()
        for i in sorted(range(1, N), key=lambda i: -hops(ORDER[i])):
            pl.semaphore_signal(barrier, inc=1, device_id=self.target(i), device_id_type=LOGICAL)
        return barrier


def ints(shape, dim):
    return lax.broadcasted_iota(jnp.int32, shape, dim)


def split(owner, target, ahead):
    mine = owner == target
    earlier = dot(jnp.where(mine, 1.0, 0.0), ahead, NN)
    return jnp.where(mine & (earlier < 0.5), 1.0, 0.0), jnp.where(mine & (earlier == 1.0), 1.0, 0.0)


def bounded(i, n):
    return jnp.clip(i, 0, n - 1)


def normed(x, gains):
    x = x.astype(jnp.float32)
    meansq = jnp.mean(x * x, axis=-1, keepdims=True)
    return (x * lax.rsqrt(meansq + norm_eps) * gains).astype(jnp.bfloat16)


def weighed(y, w0, w1):
    return (y.astype(jnp.float32) * jnp.where(ints((2, 1), 0) == 0, w0, w1)).astype(jnp.bfloat16)


def whole(ref, sem):
    return pltpu.make_async_copy(ref, ref, sem)


def remote(src, dst, send_sem, recv_sem, to):
    return pltpu.make_async_remote_copy(src_ref=src, dst_ref=dst, send_sem=send_sem, recv_sem=recv_sem,
                                        device_id=to, device_id_type=LOGICAL)


def exchange(hidden, gain, prompt_of, lengths, reward, order, rows_out, table_out, flag_out, adv_out, weights_out,
             hbuf, gbuf, obuf, tab, itab, stab, jtab, ttab, meta, meta_in, extra, piece_in, part, part_in, extra_in,
             send, recv, wtab, wsm, flag,
             in_sem, tab_sem, meta_send, meta_recv, piece_send, piece_recv, part_send, part_recv,
             send_sem, recv_sem):
    fetch_tab = [pltpu.make_async_copy(ref, tab.at[pl.ds(k, 1)], in_sem.at[2 + k])
                 for k, ref in enumerate((prompt_of, lengths, reward))]
    fetch_tab.append(pltpu.make_async_copy(order, obuf, in_sem.at[5]))
    fetch_rows = pltpu.make_async_copy(hidden, hbuf, in_sem.at[0])
    fetch_gain = pltpu.make_async_copy(gain, gbuf, in_sem.at[1])
    for copy in fetch_tab:
        copy.start()
    fetch_rows.start()
    fetch_gain.start()
    place = Place()
    me = place.me
    barrier = place.greet()
    for copy in fetch_tab:
        copy.wait()

    rows, lanes = ints((N, N), 0), ints((N, N), 1)
    row8, lane8 = ints((8, N), 0), ints((8, N), 1)
    lane1 = ints((1, N), 1)
    lanef = lane8.astype(jnp.float32)
    by_sublane, by_lane = obuf[0:N], obuf[N:N + 8]
    target = place.all(by_sublane, 1)

    prompt, length, level = tab[0:1], tab[1:2], tab[2:3]
    owner, label = prompt // OWN, lax.rem(prompt, OWN) + 1
    slot0, slot1 = split(owner, target, jnp.where(rows < lanes, 1.0, 0.0))
    twice = jnp.sum(slot1, axis=0, keepdims=True)
    spare = jnp.sum(twice, axis=1, keepdims=True)
    spare_row = jnp.sum(twice * lane1.astype(jnp.float32), axis=1, keepdims=True)
    spare_to = jnp.where(spare > 0.5, jnp.sum(twice * owner.astype(jnp.float32), axis=1, keepdims=True), -1.0)
    itab[...] = jnp.where(row8 == 0, dot(lanef, slot0, NT), spare_row).astype(jnp.int32)
    to_scalar = pltpu.make_async_copy(itab, stab, tab_sem.at[0])
    to_scalar.start()
    zero = jnp.zeros((N, N), jnp.int32)
    told = jnp.where(rows == 0, label, jnp.where(rows == 1, level, jnp.where(rows == 2, length, zero)))
    told1 = jnp.where(rows == 3, label, jnp.where(rows == 4, level, jnp.where(rows == 5, length, zero)))
    meta[...] = (dot(slot0, told.astype(jnp.float32), NT) + dot(slot1, told1.astype(jnp.float32), NT)
                 + jnp.where(lanes == 6, spare_to, jnp.where(lanes == 7, spare, 0.0))).astype(jnp.int32)
    to_scalar.wait()
    fetch_gain.wait()
    gains = gbuf[...]
    fetch_rows.wait()
    extra[...] = normed(hbuf[bounded(stab[1, 0], N)], gains)

    def pack(i):
        if i < N:
            send[i] = normed(hbuf[bounded(stab[0, i], N)], gains)

    def ship(i):
        remote(send.at[i], recv.at[i], send_sem, recv_sem.at[i // BATCH], place.target(i)).start()

    def hand(r):
        t = lax.rem(me // 4 + r, PIECES)
        return extra.at[:, pl.ds(pl.multiple_of(t * 128, 128), 128)], 4 * t

    relay = lax.rem(me, 4) == 0
    for i in range(READY):
        pack(i)
    pltpu.make_async_copy(send.at[0], recv.at[0], recv_sem.at[0]).start()
    pltpu.make_async_copy(meta.at[pl.ds(0, 1)], meta_in.at[pl.ds(0, 1)], meta_recv).start()

    @pl.when(relay)
    def _():
        pltpu.make_async_copy(hand(0)[0], piece_in.at[me], piece_recv).start()

    pl.semaphore_wait(barrier, N - 1)

    for i in range(1, FIRST):
        ship(i)
    for i in range(1, N):
        remote(meta.at[pl.ds(i, 1)], meta_in.at[pl.ds(i, 1)], meta_send, meta_recv, place.target(i)).start()

    @pl.when(jnp.logical_not(relay))
    def _():
        tile, to = hand(0)
        remote(tile, piece_in.at[me], piece_send, piece_recv, to).start()
    for r in range(1, PIECES):
        tile, to = hand(r)
        remote(tile, piece_in.at[me], piece_send, piece_recv, to).start()
    for i in range(FIRST, EARLY):
        pack(i - FIRST + READY)
        ship(i)

    whole(meta_in, meta_recv).wait()
    told_in = meta_in[...].astype(jnp.float32)
    by_step = dot(jnp.where(row8 == lane8, 1.0, 0.0), told_in, NT)
    label0, label1, to1, spares = by_step[0:1], by_step[3:4], by_step[6:7], by_step[7:8]
    source = place.all(by_lane[0:1], -1)

    goes = to1 == target.astype(jnp.float32)
    jtab[...] = dot(place.all(by_lane, -1).astype(jnp.float32), jnp.where(goes, 1.0, 0.0), NT).astype(jnp.int32)
    to_scalar = pltpu.make_async_copy(jtab, ttab, tab_sem.at[0])
    to_scalar.start()
    here = jnp.where(to1 == me.astype(jnp.float32), 1.0, 0.0)

    ahead = jnp.where(place.all(by_sublane, -1) < source, 1.0, 0.0)
    group = (rows // G + 1).astype(jnp.float32)
    rank = lax.rem(rows, G).astype(jnp.float32)
    in0, in1 = jnp.where(label0 == group, 1.0, 0.0), jnp.where(label1 == group, 1.0, 0.0)
    passed = dot(in0 + in1, ahead, NN)
    take0 = jnp.where((in0 > 0.5) & (passed == rank), 1.0, 0.0)
    take1 = jnp.where((in1 > 0.5) & (passed + in0 == rank), 1.0, 0.0)

    crowd = jnp.sum(jnp.where(goes, 1.0, 0.0), axis=1, keepdims=True)
    worst = jnp.maximum(jnp.max(crowd, axis=0, keepdims=True), jnp.max(spares, axis=1, keepdims=True))
    facts0 = jnp.where(row8 == 0, by_step[1:2], jnp.where(row8 == 1, by_step[2:3], lanef))
    facts1 = jnp.where(row8 == 0, by_step[4:5], jnp.where(row8 == 1, by_step[5:6], jnp.where(row8 == 2, 1.0 * N, lanef + N)))
    facts = dot(facts0, take0, NT) + dot(facts1, take1, NT)

    flag[...] = jnp.where(worst > 1.5, 1, 0)
    flag_copy = pltpu.make_async_copy(flag, flag_out, in_sem.at[0])
    flag_copy.start()
    to_scalar.wait()

    @pl.when(relay)
    def _():
        whole(piece_in, piece_recv).wait()
        for i in range(N):
            part[i] = piece_in[bounded(ttab[0, i], N)]
        for i in range(EARLY, EARLY + LEAD):
            ship(i)
        pltpu.make_async_copy(part.at[0], part_in.at[me // 4], part_recv).start()
        for i in range(1, N):
            remote(part.at[i], part_in.at[me // 4], part_send, part_recv, place.target(i)).start()

    @pl.when(jnp.logical_not(relay))
    def _():
        for i in range(EARLY, EARLY + LEAD):
            ship(i)
    for i in range(EARLY + LEAD, N):
        pack(i - FIRST - LEAD + READY)
        ship(i)

    same = jnp.where(rows // G == lanes // G, 1.0, 0.0)
    mean = dot(facts, same, NN) * (1.0 / G)
    centred = facts - mean
    spread = jnp.sqrt(dot(centred * centred, same, NN, exact=True) * (1.0 / G))
    adv = centred[0:1] / jnp.maximum(spread[0:1], 1.0)
    count = facts[1:2]
    weight = adv / count
    wrows = jnp.where(row8 == 0, weight, jnp.where((row8 == 1) & (count > 1.5), weight, 0.0))
    by0, by1 = dot(wrows, take0, NN, exact=True), dot(wrows, take1, NN, exact=True)
    wtab[0] = by0
    wtab[1] = jnp.sum(by1 * here, axis=1, keepdims=True) + jnp.zeros((8, N), jnp.float32)
    to_scalar = pltpu.make_async_copy(wtab, wsm, tab_sem.at[1])
    to_scalar.start()
    weights_out[...] = by1
    table_out[...] = jnp.where(row8 == 0, facts[2:3], facts[3:4]).astype(jnp.int32)
    adv_out[...] = adv
    to_scalar.wait()

    def settle(g, _):
        whole(recv.at[pl.ds(0, BATCH)], recv_sem.at[g]).wait()
        for k in range(BATCH):
            i = g * BATCH + k
            rows_out[i] = weighed(recv[i], wsm[0, 0, i], wsm[0, 1, i])
        return 0
    lax.fori_loop(0, LATE, settle, 0)

    whole(part_in, part_recv).wait()
    for t in range(PIECES):
        extra_in[:, pl.ds(t * 128, 128)] = part_in[t]
    rows_out[N] = weighed(extra_in[...], wsm[1, 0, 0], wsm[1, 1, 0])
    lax.fori_loop(LATE, N // BATCH, settle, 0)

    whole(meta.at[pl.ds(0, N - 1)], meta_send).wait()
    whole(send.at[pl.ds(0, N - 1)], send_sem).wait()
    flag_copy.wait()

    @pl.when(relay)
    def _():
        whole(piece_in.at[pl.ds(0, PIECES - 1)], piece_send).wait()
        whole(part.at[pl.ds(0, N - 1)], part_send).wait()

    @pl.when(jnp.logical_not(relay))
    def _():
        whole(piece_in.at[pl.ds(0, PIECES)], piece_send).wait()


def second(hidden, gain, prompt_of, weights, order, rows_out, hbuf, gbuf, obuf, tab, itab, stab, send, recv, wsm,
           in_sem, tab_sem, send_sem, recv_sem):
    copies = [pltpu.make_async_copy(a, b, in_sem.at[k]) for k, (a, b) in enumerate(
        ((hidden, hbuf), (gain, gbuf), (prompt_of, tab.at[pl.ds(0, 1)]), (weights, wsm), (order, obuf)))]
    for copy in copies:
        copy.start()
    place = Place()
    barrier = place.greet()
    for copy in copies:
        copy.wait()
    rows, lanes = ints((N, N), 0), ints((N, N), 1)
    slot1 = split(tab[0:1] // OWN, place.all(obuf[0:N], 1), jnp.where(rows < lanes, 1.0, 0.0))[1]
    itab[...] = dot(ints((8, N), 1).astype(jnp.float32), slot1, NT).astype(jnp.int32)
    to_scalar = pltpu.make_async_copy(itab, stab, tab_sem)
    to_scalar.start()
    to_scalar.wait()
    pl.semaphore_wait(barrier, N - 1)

    def pack(i, _):
        send[i] = hbuf[bounded(stab[0, i], N)]
        return 0
    lax.fori_loop(0, N, pack, 0)
    pltpu.make_async_copy(send.at[0], recv.at[0], recv_sem).start()

    for i in range(1, N):
        remote(send.at[i], recv.at[i], send_sem, recv_sem, place.target(i)).start()
    whole(recv, recv_sem).wait()
    gains = gbuf[...]

    def settle(i, _):
        rows_out[i] = weighed(normed(recv[i], gains), wsm[0, i], wsm[1, i])
        return 0
    lax.fori_loop(0, N, settle, 0)
    whole(send.at[pl.ds(0, N - 1)], send_sem).wait()


def arrange(table, adv_in, rows_in, out, adv_out, sem, adv_sem):
    put_adv = pltpu.make_async_copy(adv_in, adv_out, adv_sem)
    put_adv.start()
    for q in range(N):
        pltpu.make_async_copy(rows_in.at[bounded(table[0, q], N + 1)], out.at[q], sem).start()
    whole(out, sem).wait()
    put_adv.wait()


def arrange_both(table, adv_in, rows_in, more_in, out, adv_out, sem, adv_sem):
    put_adv = pltpu.make_async_copy(adv_in, adv_out, adv_sem)
    put_adv.start()

    def put(q, _):
        i = bounded(table[1, q], 2 * N)

        @pl.when(i < N)
        def _():
            pltpu.make_async_copy(rows_in.at[i], out.at[q], sem).start()

        @pl.when(i >= N)
        def _():
            pltpu.make_async_copy(more_in.at[i - N], out.at[q], sem).start()
        return 0
    lax.fori_loop(0, N, put, 0)
    whole(out, sem).wait()
    put_adv.wait()


def on_device(hidden, norm_gain, prompt_of, lengths, reward_level):
    count, window, features = hidden.shape
    bf16, f32, i32 = jnp.bfloat16, jnp.float32, jnp.int32
    shape = jax.ShapeDtypeStruct
    any_space = pl.BlockSpec(memory_space=pl.ANY)
    vmem = pl.BlockSpec(memory_space=pltpu.VMEM)
    dma = pltpu.SemaphoreType.DMA
    block = pltpu.VMEM((N, window, features), bf16)
    square, strip = pltpu.VMEM((N, N), i32), pltpu.VMEM((8, N), i32)
    gains = pltpu.VMEM((1, features), f32)
    steps = pltpu.VMEM((N + 8, N), i32)
    order = jnp.asarray(np.concatenate([np.repeat(np.array(ORDER, np.int32)[:, None], N, 1), np.repeat(np.array([ORDER], np.int32), 8, 0)]))
    gain, prompt, length, level = (a.reshape(1, a.shape[0]) for a in (norm_gain, prompt_of, lengths, reward_level))
    rows, table, flag, adv, weights = pl.pallas_call(
        exchange,
        out_shape=(shape((N + 1, window, features), bf16), shape((8, N), i32), shape((1, 1), i32),
                   shape((1, N), f32), shape((8, N), f32)),
        in_specs=[any_space] * 6,
        out_specs=(vmem, vmem, any_space, vmem, vmem),
        scratch_shapes=[
            block, gains, steps, strip, strip, pltpu.SMEM((8, N), i32), strip, pltpu.SMEM((8, N), i32), square, square,
            pltpu.VMEM((window, features), bf16), pltpu.VMEM((N, window, 128), bf16),
            pltpu.VMEM((N, window, 128), bf16), pltpu.VMEM((PIECES, window, 128), bf16), pltpu.VMEM((window, features), bf16),
            block, block, pltpu.VMEM((2, 8, N), f32), pltpu.SMEM((2, 8, N), f32), pltpu.VMEM((1, 1), i32),
            dma((6,)), dma((2,)), dma, dma, dma, dma, dma, dma, dma, dma((N // BATCH,))],
        compiler_params=pltpu.CompilerParams(collective_id=0, has_side_effects=True),
        name="exchange",
    )(hidden, gain, prompt, length, level, order)

    def put(kernel, *row_blocks):
        return pl.pallas_call(
            kernel,
            out_shape=(shape((N, window, features), bf16), shape((1, N), f32)),
            in_specs=[pl.BlockSpec(memory_space=pltpu.SMEM)] + [any_space] * (1 + len(row_blocks)),
            out_specs=(any_space, any_space),
            scratch_shapes=[dma, dma],
            name=kernel.__name__,
        )(table, adv, *row_blocks)

    def few(_):
        return put(arrange, rows)

    def many(_):
        more = pl.pallas_call(
            second,
            out_shape=shape((N, window, features), bf16),
            in_specs=[any_space] * 5,
            out_specs=vmem,
            scratch_shapes=[
                block, gains, steps, strip, strip, pltpu.SMEM((8, N), i32), block, block, pltpu.SMEM((8, N), f32),
                dma((5,)), dma, dma, dma],
            compiler_params=pltpu.CompilerParams(collective_id=1, has_side_effects=True, vmem_limit_bytes=24 << 20),
            name="second",
        )(hidden, gain, prompt, weights, order)
        return put(arrange_both, rows, more)

    out, adv = lax.switch(flag[0, 0], (few, many), 0)
    return out, adv.reshape(N)


def solution(mesh):
    spec = P(AXES)
    return jax.shard_map(
        on_device, mesh=mesh, in_specs=(P(AXES, None, None), P(), spec, spec, spec),
        out_specs=(P(AXES, None, None), spec), check_vma=False)
```

```python
import functools
import random

import jax
import jax.numpy as jnp
import numpy as np
from jax import lax
from jax.experimental import pallas as pl
from jax.experimental.pallas import tpu as pltpu
from jax.sharding import PartitionSpec as P

LOGICAL = pl.DeviceIdType.LOGICAL
AXES = ("gx", "gy", "gz")
N = 128
G = 16
OWN = 8
PIECES = 32
RAW = 80
EARLY = 80
LEAD = 4
BATCH = 8
LATE = 15
SEED = 0
norm_eps = 1e-05

NT = (((1,), (1,)), ((), ()))
NN = (((1,), (0,)), ((), ()))


def hops(o):
    return sum(min(k, 4 - k) for k in (o // 32, o // 8 % 4, o // 2 % 4))


def make_order(seed):
    rest = list(range(1, N))
    random.Random(seed).shuffle(rest)
    return [0] + sorted(rest, key=lambda o: hops(o) < 3)


ORDER = make_order(SEED)


def dot(a, b, dims, exact=False):
    if exact:
        return lax.dot_general(a, b, dims, precision=lax.Precision.HIGHEST,
                               preferred_element_type=jnp.float32)
    return lax.dot_general(a.astype(jnp.bfloat16), b.astype(jnp.bfloat16), dims,
                           preferred_element_type=jnp.float32)


class Place:
    def __init__(self):
        self.x, self.y, gz = lax.axis_index("gx"), lax.axis_index("gy"), lax.axis_index("gz")
        self.z, self.core = gz // 2, lax.rem(gz, 2)
        self.me = self.x * 32 + self.y * 8 + gz
        self.xs = [lax.rem(self.x + k, 4) * 32 for k in range(4)]
        self.ys = [lax.rem(self.y + k, 4) * 8 for k in range(4)]
        self.zs = [lax.rem(self.z + k, 4) * 2 for k in range(4)]
        self.cores = [lax.rem(self.core + k, 2) for k in range(2)]
        self.zc = [[z + c for c in self.cores] for z in self.zs]
        self.xy = [[a + b for b in self.ys] for a in self.xs]

    def target(self, i):
        o = ORDER[i]
        return self.xy[o // 32][o // 8 % 4] + self.zc[o // 2 % 4][o % 2]

    def all(self, o, sign):
        return ((((self.x + sign * (o >> 5)) & 3) << 5) + (((self.y + sign * ((o >> 3) & 3)) & 3) << 3)
                + (((self.z + sign * ((o >> 1) & 3)) & 3) << 1) + ((self.core + o) & 1))

    def greet(self):
        barrier = pltpu.get_barrier_semaphore()
        for i in sorted(range(1, N), key=lambda i: -hops(ORDER[i])):
            pl.semaphore_signal(barrier, inc=1, device_id=self.target(i), device_id_type=LOGICAL)
        return barrier


def ints(shape, dim):
    return lax.broadcasted_iota(jnp.int32, shape, dim)


def split(owner, target, ahead):
    mine = owner == target
    earlier = dot(jnp.where(mine, 1.0, 0.0), ahead, NN)
    return jnp.where(mine & (earlier < 0.5), 1.0, 0.0), jnp.where(mine & (earlier == 1.0), 1.0, 0.0)


def bounded(i, n):
    return jnp.clip(i, 0, n - 1)


def normed(x, gains):
    x = x.astype(jnp.float32)
    meansq = jnp.mean(x * x, axis=-1, keepdims=True)
    return (x * lax.rsqrt(meansq + norm_eps) * gains).astype(jnp.bfloat16)


def weighed(y, w0, w1):
    return (y.astype(jnp.float32) * jnp.where(ints((2, 1), 0) == 0, w0, w1)).astype(jnp.bfloat16)


def whole(ref, sem):
    return pltpu.make_async_copy(ref, ref, sem)


def remote(src, dst, send_sem, recv_sem, to):
    return pltpu.make_async_remote_copy(src_ref=src, dst_ref=dst, send_sem=send_sem, recv_sem=recv_sem,
                                        device_id=to, device_id_type=LOGICAL)


def exchange(hidden, gain, prompt_of, lengths, reward, order, rows_out, table_out, flag_out, adv_out, weights_out,
             hbuf, gbuf, obuf, tab, itab, stab, jtab, ttab, meta, meta_in, share, share_in, extra, piece_in, part, part_in, extra_in,
             send, recv, wtab, wsm, flag,
             in_sem, tab_sem, meta_send, meta_recv, share_send, share_recv, piece_send, piece_recv, part_send, part_recv,
             send_sem, recv_sem):
    fetch_tab = [pltpu.make_async_copy(ref, tab.at[pl.ds(k, 1)], in_sem.at[2 + k])
                 for k, ref in enumerate((prompt_of, lengths, reward))]
    fetch_tab.append(pltpu.make_async_copy(order, obuf, in_sem.at[5]))
    fetch_rows = pltpu.make_async_copy(hidden, hbuf, in_sem.at[0])
    fetch_gain = pltpu.make_async_copy(gain, gbuf, in_sem.at[1])
    for copy in fetch_tab:
        copy.start()
    fetch_rows.start()
    fetch_gain.start()
    place = Place()
    me = place.me
    barrier = place.greet()
    for copy in fetch_tab:
        copy.wait()

    rows, lanes = ints((N, N), 0), ints((N, N), 1)
    row8, lane8 = ints((8, N), 0), ints((8, N), 1)
    lane1 = ints((1, N), 1)
    lanef = lane8.astype(jnp.float32)
    by_sublane, by_lane = obuf[0:N], obuf[N:N + 8]
    target = place.all(by_sublane, 1)

    prompt, length, level = tab[0:1], tab[1:2], tab[2:3]
    owner, label = prompt // OWN, lax.rem(prompt, OWN) + 1
    slot0, slot1 = split(owner, rows, jnp.where(rows < lanes, 1.0, 0.0))
    once, twice = jnp.sum(slot0, axis=0, keepdims=True), jnp.sum(slot1, axis=0, keepdims=True)
    spare = jnp.sum(twice, axis=1, keepdims=True)
    spare_row = jnp.sum(twice * lane1.astype(jnp.float32), axis=1, keepdims=True)
    spare_to = jnp.where(spare > 0.5, jnp.sum(twice * owner.astype(jnp.float32), axis=1, keepdims=True), -1.0)
    itab[...] = jnp.where(row8 == 0, dot(lanef, slot0, NT), spare_row).astype(jnp.int32)
    to_scalar = pltpu.make_async_copy(itab, stab, tab_sem.at[0])
    to_scalar.start()

    number, member = rows & 7, (rows >> 3) == (owner & 3)
    zero = jnp.zeros((N, N), jnp.int32)
    told0 = jnp.where(number == 0, label, jnp.where(number == 1, level, jnp.where(number == 2, length, zero)))
    told1 = jnp.where(number == 3, label, jnp.where(number == 4, level, jnp.where(number == 5, length, zero)))
    told0, told1 = (jnp.where(member, told, zero).astype(jnp.float32) for told in (told0, told1))
    cell = jnp.where((owner >> 2) == ints((PIECES, N), 0), 1.0, 0.0)
    lane32 = ints((PIECES, N), 1)
    meta[...] = (dot(cell * once, told0, NT) + dot(cell * twice, told1, NT)
                 + jnp.where(lane32 == 32, spare_to, jnp.where(lane32 == 33, spare, 0.0))).astype(jnp.int32)
    to_scalar.wait()
    fetch_gain.wait()
    gains = gbuf[...]
    fetch_rows.wait()
    extra[...] = normed(hbuf[bounded(stab[1, 0], N)], gains)

    def pack(i):
        if i < N:
            row = hbuf[bounded(stab[0, place.target(i)], N)]
            send[i] = row if i < RAW else normed(row, gains)

    def ship(i):
        remote(send.at[i], recv.at[i], send_sem, recv_sem.at[i // BATCH], place.target(i)).start()

    def hand(r, copy):
        t = lax.rem(me // 4 + r, PIECES)
        copy(meta.at[pl.ds(t, 1)], meta_in.at[pl.ds(me, 1)], meta_send, meta_recv, 4 * t)
        copy(extra.at[:, pl.ds(pl.multiple_of(t * 128, 128), 128)], piece_in.at[me], piece_send, piece_recv, 4 * t)

    def away(src, dst, send_sem, recv_sem, to):
        remote(src, dst, send_sem, recv_sem, to).start()

    def at_home(src, dst, send_sem, recv_sem, to):
        pltpu.make_async_copy(src, dst, recv_sem).start()

    relay = lax.rem(me, 4) == 0
    for i in range(RAW):
        pack(i)
    pltpu.make_async_copy(send.at[0], recv.at[0], recv_sem.at[0]).start()

    @pl.when(relay)
    def _():
        hand(0, at_home)

    pl.semaphore_wait(barrier, N - 1)

    @pl.when(jnp.logical_not(relay))
    def _():
        hand(0, away)
    for r in range(1, PIECES):
        hand(r, away)
    for i in range(1, RAW):
        ship(i)
    for i in range(RAW, EARLY + LEAD):
        pack(i)
        if i >= RAW + LEAD:
            ship(i - LEAD)

    @pl.when(relay)
    def _():
        whole(meta_in, meta_recv).wait()
        told_in = meta_in[...].astype(jnp.float32)
        for u in range(4):
            wanted = jnp.where(row8 < 6, row8 + 8 * u, row8 + 26)
            share[u] = dot(jnp.where(lane8 == wanted, 1.0, 0.0), told_in, NT).astype(jnp.int32)
        goes = share[0, 6:7, :] == target
        jtab[...] = dot(lanef, jnp.where(goes, 1.0, 0.0), NT).astype(jnp.int32)
        to_scalar = pltpu.make_async_copy(jtab, ttab, tab_sem.at[0])
        to_scalar.start()
        to_scalar.wait()
        pltpu.make_async_copy(share.at[0], share_in, share_recv).start()
        for u in range(1, 4):
            remote(share.at[u], share_in, share_send, share_recv, me + u).start()
        whole(piece_in, piece_recv).wait()
        for i in range(N):
            part[i] = piece_in[bounded(ttab[0, i], N)]
        pltpu.make_async_copy(part.at[0], part_in.at[me // 4], part_recv).start()
        for i in range(1, N):
            remote(part.at[i], part_in.at[me // 4], part_send, part_recv, place.target(i)).start()

    for i in range(EARLY, N):
        pack(i + LEAD)
        ship(i)

    whole(share_in, share_recv).wait()
    source = place.all(by_lane[0:1], -1)
    by_step = dot(share_in[...].astype(jnp.float32), jnp.where(rows == source, 1.0, 0.0), NN)
    label0, label1, to1, spares = by_step[0:1], by_step[3:4], by_step[6:7], by_step[7:8]
    goes = to1 == rows.astype(jnp.float32)
    here = jnp.where(to1 == me.astype(jnp.float32), 1.0, 0.0)

    ahead = jnp.where(place.all(by_sublane, -1) < source, 1.0, 0.0)
    group = (rows // G + 1).astype(jnp.float32)
    rank = lax.rem(rows, G).astype(jnp.float32)
    in0, in1 = jnp.where(label0 == group, 1.0, 0.0), jnp.where(label1 == group, 1.0, 0.0)
    passed = dot(in0 + in1, ahead, NN)
    take0 = jnp.where((in0 > 0.5) & (passed == rank), 1.0, 0.0)
    take1 = jnp.where((in1 > 0.5) & (passed + in0 == rank), 1.0, 0.0)

    crowd = jnp.sum(jnp.where(goes, 1.0, 0.0), axis=1, keepdims=True)
    worst = jnp.maximum(jnp.max(crowd, axis=0, keepdims=True), jnp.max(spares, axis=1, keepdims=True))
    facts0 = jnp.where(row8 == 0, by_step[1:2], jnp.where(row8 == 1, by_step[2:3], lanef))
    facts1 = jnp.where(row8 == 0, by_step[4:5], jnp.where(row8 == 1, by_step[5:6], jnp.where(row8 == 2, 1.0 * N, lanef + N)))
    facts = dot(facts0, take0, NT) + dot(facts1, take1, NT)

    flag[...] = jnp.where(worst > 1.5, 1, 0)
    flag_copy = pltpu.make_async_copy(flag, flag_out, in_sem.at[0])
    flag_copy.start()
    same = jnp.where(rows // G == lanes // G, 1.0, 0.0)
    mean = dot(facts, same, NN) * (1.0 / G)
    centred = facts - mean
    spread = jnp.sqrt(dot(centred * centred, same, NN, exact=True) * (1.0 / G))
    adv = centred[0:1] / jnp.maximum(spread[0:1], 1.0)
    count = facts[1:2]
    weight = adv / count
    wrows = jnp.where(row8 == 0, weight, jnp.where((row8 == 1) & (count > 1.5), weight, 0.0))
    by0, by1 = dot(wrows, take0, NN, exact=True), dot(wrows, take1, NN, exact=True)
    wtab[0] = by0
    wtab[1] = jnp.sum(by1 * here, axis=1, keepdims=True) + jnp.zeros((8, N), jnp.float32)
    to_scalar = pltpu.make_async_copy(wtab, wsm, tab_sem.at[1])
    to_scalar.start()
    weights_out[...] = by1
    table_out[...] = jnp.where(row8 == 0, facts[2:3], facts[3:4]).astype(jnp.int32)
    adv_out[...] = adv
    to_scalar.wait()

    def settle(raw, g, _):
        whole(recv.at[pl.ds(0, BATCH)], recv_sem.at[g]).wait()
        for k in range(BATCH):
            i = g * BATCH + k
            row = normed(recv[i], gains) if raw else recv[i]
            rows_out[i] = weighed(row, wsm[0, 0, i], wsm[0, 1, i])
        return 0
    lax.fori_loop(0, RAW // BATCH, functools.partial(settle, True), 0)
    lax.fori_loop(RAW // BATCH, LATE, functools.partial(settle, False), 0)

    whole(part_in, part_recv).wait()
    for t in range(PIECES):
        extra_in[:, pl.ds(t * 128, 128)] = part_in[t]
    rows_out[N] = weighed(extra_in[...], wsm[1, 0, 0], wsm[1, 1, 0])
    lax.fori_loop(LATE, N // BATCH, functools.partial(settle, False), 0)

    whole(send.at[pl.ds(0, N - 1)], send_sem).wait()
    flag_copy.wait()

    @pl.when(relay)
    def _():
        whole(meta.at[pl.ds(0, PIECES - 1)], meta_send).wait()
        whole(piece_in.at[pl.ds(0, PIECES - 1)], piece_send).wait()
        whole(share.at[pl.ds(0, 3)], share_send).wait()
        whole(part.at[pl.ds(0, N - 1)], part_send).wait()

    @pl.when(jnp.logical_not(relay))
    def _():
        whole(meta, meta_send).wait()
        whole(piece_in.at[pl.ds(0, PIECES)], piece_send).wait()


def second(hidden, gain, prompt_of, weights, order, rows_out, hbuf, gbuf, obuf, tab, itab, stab, send, recv, wsm,
           in_sem, tab_sem, send_sem, recv_sem):
    copies = [pltpu.make_async_copy(a, b, in_sem.at[k]) for k, (a, b) in enumerate(
        ((hidden, hbuf), (gain, gbuf), (prompt_of, tab.at[pl.ds(0, 1)]), (weights, wsm), (order, obuf)))]
    for copy in copies:
        copy.start()
    place = Place()
    barrier = place.greet()
    for copy in copies:
        copy.wait()
    rows, lanes = ints((N, N), 0), ints((N, N), 1)
    slot1 = split(tab[0:1] // OWN, place.all(obuf[0:N], 1), jnp.where(rows < lanes, 1.0, 0.0))[1]
    itab[...] = dot(ints((8, N), 1).astype(jnp.float32), slot1, NT).astype(jnp.int32)
    to_scalar = pltpu.make_async_copy(itab, stab, tab_sem)
    to_scalar.start()
    to_scalar.wait()
    pl.semaphore_wait(barrier, N - 1)

    def pack(i, _):
        send[i] = hbuf[bounded(stab[0, i], N)]
        return 0
    lax.fori_loop(0, N, pack, 0)
    pltpu.make_async_copy(send.at[0], recv.at[0], recv_sem).start()

    for i in range(1, N):
        remote(send.at[i], recv.at[i], send_sem, recv_sem, place.target(i)).start()
    whole(recv, recv_sem).wait()
    gains = gbuf[...]

    def settle(i, _):
        rows_out[i] = weighed(normed(recv[i], gains), wsm[0, i], wsm[1, i])
        return 0
    lax.fori_loop(0, N, settle, 0)
    whole(send.at[pl.ds(0, N - 1)], send_sem).wait()


def arrange(table, adv_in, rows_in, out, adv_out, sem, adv_sem):
    put_adv = pltpu.make_async_copy(adv_in, adv_out, adv_sem)
    put_adv.start()
    for q in range(N):
        pltpu.make_async_copy(rows_in.at[bounded(table[0, q], N + 1)], out.at[q], sem).start()
    whole(out, sem).wait()
    put_adv.wait()


def arrange_both(table, adv_in, rows_in, more_in, out, adv_out, sem, adv_sem):
    put_adv = pltpu.make_async_copy(adv_in, adv_out, adv_sem)
    put_adv.start()

    def put(q, _):
        i = bounded(table[1, q], 2 * N)

        @pl.when(i < N)
        def _():
            pltpu.make_async_copy(rows_in.at[i], out.at[q], sem).start()

        @pl.when(i >= N)
        def _():
            pltpu.make_async_copy(more_in.at[i - N], out.at[q], sem).start()
        return 0
    lax.fori_loop(0, N, put, 0)
    whole(out, sem).wait()
    put_adv.wait()


def on_device(hidden, norm_gain, prompt_of, lengths, reward_level):
    count, window, features = hidden.shape
    bf16, f32, i32 = jnp.bfloat16, jnp.float32, jnp.int32
    shape = jax.ShapeDtypeStruct
    any_space = pl.BlockSpec(memory_space=pl.ANY)
    vmem = pl.BlockSpec(memory_space=pltpu.VMEM)
    dma = pltpu.SemaphoreType.DMA
    block = pltpu.VMEM((N, window, features), bf16)
    square, strip = pltpu.VMEM((N, N), i32), pltpu.VMEM((8, N), i32)
    gains = pltpu.VMEM((1, features), f32)
    steps = pltpu.VMEM((N + 8, N), i32)
    order = jnp.asarray(np.concatenate([np.repeat(np.array(ORDER, np.int32)[:, None], N, 1), np.repeat(np.array([ORDER], np.int32), 8, 0)]))
    gain, prompt, length, level = (a.reshape(1, a.shape[0]) for a in (norm_gain, prompt_of, lengths, reward_level))
    rows, table, flag, adv, weights = pl.pallas_call(
        exchange,
        out_shape=(shape((N + 1, window, features), bf16), shape((8, N), i32), shape((1, 1), i32),
                   shape((1, N), f32), shape((8, N), f32)),
        in_specs=[any_space] * 6,
        out_specs=(vmem, vmem, any_space, vmem, vmem),
        scratch_shapes=[
            block, gains, steps, strip, strip, pltpu.SMEM((8, N), i32), strip, pltpu.SMEM((8, N), i32),
            pltpu.VMEM((PIECES, N), i32), square, pltpu.VMEM((4, 8, N), i32), strip,
            pltpu.VMEM((window, features), bf16), pltpu.VMEM((N, window, 128), bf16),
            pltpu.VMEM((N, window, 128), bf16), pltpu.VMEM((PIECES, window, 128), bf16), pltpu.VMEM((window, features), bf16),
            block, block, pltpu.VMEM((2, 8, N), f32), pltpu.SMEM((2, 8, N), f32), pltpu.VMEM((1, 1), i32),
            dma((6,)), dma((2,)), dma, dma, dma, dma, dma, dma, dma, dma, dma, dma((N // BATCH,))],
        compiler_params=pltpu.CompilerParams(collective_id=0, has_side_effects=True),
        name="exchange",
    )(hidden, gain, prompt, length, level, order)

    def put(kernel, *row_blocks):
        return pl.pallas_call(
            kernel,
            out_shape=(shape((N, window, features), bf16), shape((1, N), f32)),
            in_specs=[pl.BlockSpec(memory_space=pltpu.SMEM)] + [any_space] * (1 + len(row_blocks)),
            out_specs=(any_space, any_space),
            scratch_shapes=[dma, dma],
            name=kernel.__name__,
        )(table, adv, *row_blocks)

    def few(_):
        return put(arrange, rows)

    def many(_):
        more = pl.pallas_call(
            second,
            out_shape=shape((N, window, features), bf16),
            in_specs=[any_space] * 5,
            out_specs=vmem,
            scratch_shapes=[
                block, gains, steps, strip, strip, pltpu.SMEM((8, N), i32), block, block, pltpu.SMEM((8, N), f32),
                dma((5,)), dma, dma, dma],
            compiler_params=pltpu.CompilerParams(collective_id=1, has_side_effects=True, vmem_limit_bytes=24 << 20),
            name="second",
        )(hidden, gain, prompt, weights, order)
        return put(arrange_both, rows, more)

    out, adv = lax.switch(flag[0, 0], (few, many), 0)
    return out, adv.reshape(N)


def solution(mesh):
    spec = P(AXES)
    return jax.shard_map(
        on_device, mesh=mesh, in_specs=(P(AXES, None, None), P(), spec, spec, spec),
        out_specs=(P(AXES, None, None), spec), check_vma=False)
```

```python
import functools
import random

import jax
import jax.numpy as jnp
import numpy as np
from jax import lax
from jax.experimental import pallas as pl
from jax.experimental.pallas import tpu as pltpu
from jax.sharding import PartitionSpec as P

LOGICAL = pl.DeviceIdType.LOGICAL
AXES = ("gx", "gy", "gz")
N = 128
G = 16
OWN = 8
PIECES = 32
RAW = 80
EARLY = 80
LEAD = 4
BATCH = 16
LATE = 7
SEED = 0
norm_eps = 1e-05

NT = (((1,), (1,)), ((), ()))
NN = (((1,), (0,)), ((), ()))


def hops(o):
    return sum(min(k, 4 - k) for k in (o // 32, o // 8 % 4, o // 2 % 4))


def make_order(seed):
    rest = list(range(1, N))
    random.Random(seed).shuffle(rest)
    return [0] + sorted(rest, key=lambda o: hops(o) < 3)


ORDER = make_order(SEED)


def dot(a, b, dims, exact=False):
    if exact:
        return lax.dot_general(a, b, dims, precision=lax.Precision.HIGHEST,
                               preferred_element_type=jnp.float32)
    return lax.dot_general(a.astype(jnp.bfloat16), b.astype(jnp.bfloat16), dims,
                           preferred_element_type=jnp.float32)


class Place:
    def __init__(self):
        self.x, self.y, gz = lax.axis_index("gx"), lax.axis_index("gy"), lax.axis_index("gz")
        self.z, self.core = gz // 2, lax.rem(gz, 2)
        self.me = self.x * 32 + self.y * 8 + gz
        self.xs = [lax.rem(self.x + k, 4) * 32 for k in range(4)]
        self.ys = [lax.rem(self.y + k, 4) * 8 for k in range(4)]
        self.zs = [lax.rem(self.z + k, 4) * 2 for k in range(4)]
        self.cores = [lax.rem(self.core + k, 2) for k in range(2)]
        self.zc = [[z + c for c in self.cores] for z in self.zs]
        self.xy = [[a + b for b in self.ys] for a in self.xs]

    def target(self, i):
        o = ORDER[i]
        return self.xy[o // 32][o // 8 % 4] + self.zc[o // 2 % 4][o % 2]

    def all(self, o, sign):
        return ((((self.x + sign * (o >> 5)) & 3) << 5) + (((self.y + sign * ((o >> 3) & 3)) & 3) << 3)
                + (((self.z + sign * ((o >> 1) & 3)) & 3) << 1) + ((self.core + o) & 1))

    def greet(self):
        barrier = pltpu.get_barrier_semaphore()
        for i in sorted(range(1, N), key=lambda i: -hops(ORDER[i])):
            pl.semaphore_signal(barrier, inc=1, device_id=self.target(i), device_id_type=LOGICAL)
        return barrier


def ints(shape, dim):
    return lax.broadcasted_iota(jnp.int32, shape, dim)


def split(owner, target, ahead):
    mine = owner == target
    earlier = dot(jnp.where(mine, 1.0, 0.0), ahead, NN)
    return jnp.where(mine & (earlier < 0.5), 1.0, 0.0), jnp.where(mine & (earlier == 1.0), 1.0, 0.0)


def bounded(i, n):
    return jnp.clip(i, 0, n - 1)


def normed(x, gains):
    x = x.astype(jnp.float32)
    meansq = jnp.mean(x * x, axis=-1, keepdims=True)
    return (x * lax.rsqrt(meansq + norm_eps) * gains).astype(jnp.bfloat16)


def weighed(y, w0, w1):
    return (y.astype(jnp.float32) * jnp.where(ints((2, 1), 0) == 0, w0, w1)).astype(jnp.bfloat16)


def whole(ref, sem):
    return pltpu.make_async_copy(ref, ref, sem)


def remote(src, dst, send_sem, recv_sem, to):
    return pltpu.make_async_remote_copy(src_ref=src, dst_ref=dst, send_sem=send_sem, recv_sem=recv_sem,
                                        device_id=to, device_id_type=LOGICAL)


def exchange(hidden, gain, prompt_of, lengths, reward, order, rows_out, table_out, flag_out, adv_out, weights_out,
             hbuf, gbuf, obuf, tab, itab, stab, jtab, ttab, meta, meta_in, share, share_in, extra, piece_in, part, part_in, extra_in,
             send, recv, wtab, wsm, flag,
             in_sem, tab_sem, meta_send, meta_recv, share_send, share_recv, piece_send, piece_recv, part_send, part_recv,
             send_sem, recv_sem):
    fetch_tab = [pltpu.make_async_copy(ref, tab.at[pl.ds(k, 1)], in_sem.at[2 + k])
                 for k, ref in enumerate((prompt_of, lengths, reward))]
    fetch_tab.append(pltpu.make_async_copy(order, obuf, in_sem.at[5]))
    fetch_rows = pltpu.make_async_copy(hidden, hbuf, in_sem.at[0])
    fetch_gain = pltpu.make_async_copy(gain, gbuf, in_sem.at[1])
    for copy in fetch_tab:
        copy.start()
    fetch_rows.start()
    fetch_gain.start()
    place = Place()
    me = place.me
    barrier = place.greet()
    for copy in fetch_tab:
        copy.wait()

    rows, lanes = ints((N, N), 0), ints((N, N), 1)
    row8, lane8 = ints((8, N), 0), ints((8, N), 1)
    lane1 = ints((1, N), 1)
    lanef = lane8.astype(jnp.float32)
    by_sublane, by_lane = obuf[0:N], obuf[N:N + 8]
    target = place.all(by_sublane, 1)

    prompt, length, level = tab[0:1], tab[1:2], tab[2:3]
    owner, label = prompt // OWN, lax.rem(prompt, OWN) + 1
    slot0, slot1 = split(owner, rows, jnp.where(rows < lanes, 1.0, 0.0))
    once, twice = jnp.sum(slot0, axis=0, keepdims=True), jnp.sum(slot1, axis=0, keepdims=True)
    spare = jnp.sum(twice, axis=1, keepdims=True)
    spare_row = jnp.sum(twice * lane1.astype(jnp.float32), axis=1, keepdims=True)
    spare_to = jnp.where(spare > 0.5, jnp.sum(twice * owner.astype(jnp.float32), axis=1, keepdims=True), -1.0)
    itab[...] = jnp.where(row8 == 0, dot(lanef, slot0, NT), spare_row).astype(jnp.int32)
    to_scalar = pltpu.make_async_copy(itab, stab, tab_sem.at[0])
    to_scalar.start()

    number, member = rows & 7, (rows >> 3) == (owner & 3)
    zero = jnp.zeros((N, N), jnp.int32)
    told0 = jnp.where(number == 0, label, jnp.where(number == 1, level, jnp.where(number == 2, length, zero)))
    told1 = jnp.where(number == 3, label, jnp.where(number == 4, level, jnp.where(number == 5, length, zero)))
    told0, told1 = (jnp.where(member, told, zero).astype(jnp.float32) for told in (told0, told1))
    cell = jnp.where((owner >> 2) == ints((PIECES, N), 0), 1.0, 0.0)
    lane32 = ints((PIECES, N), 1)
    meta[...] = (dot(cell * once, told0, NT) + dot(cell * twice, told1, NT)
                 + jnp.where(lane32 == 32, spare_to, jnp.where(lane32 == 33, spare, 0.0))).astype(jnp.int32)
    to_scalar.wait()
    fetch_gain.wait()
    gains = gbuf[...]
    fetch_rows.wait()
    extra[...] = normed(hbuf[bounded(stab[1, 0], N)], gains)

    def pack(i):
        if i < N:
            row = hbuf[bounded(stab[0, place.target(i)], N)]
            send[i] = row if i < RAW else normed(row, gains)

    def ship(i):
        remote(send.at[i], recv.at[i], send_sem, recv_sem.at[i // BATCH], place.target(i)).start()

    def hand(r, copy):
        t = lax.rem(me // 4 + r, PIECES)
        copy(meta.at[pl.ds(t, 1)], meta_in.at[pl.ds(me, 1)], meta_send, meta_recv, 4 * t)
        copy(extra.at[:, pl.ds(pl.multiple_of(t * 128, 128), 128)], piece_in.at[me], piece_send, piece_recv, 4 * t)

    def away(src, dst, send_sem, recv_sem, to):
        remote(src, dst, send_sem, recv_sem, to).start()

    def at_home(src, dst, send_sem, recv_sem, to):
        pltpu.make_async_copy(src, dst, recv_sem).start()

    relay = lax.rem(me, 4) == 0
    for i in range(RAW):
        pack(i)
    pltpu.make_async_copy(send.at[0], recv.at[0], recv_sem.at[0]).start()

    @pl.when(relay)
    def _():
        hand(0, at_home)

    pl.semaphore_wait(barrier, N - 1)

    @pl.when(jnp.logical_not(relay))
    def _():
        hand(0, away)
    for r in range(1, PIECES):
        hand(r, away)
    for i in range(1, RAW):
        ship(i)
    for i in range(RAW, EARLY + LEAD):
        pack(i)
        if i >= RAW + LEAD:
            ship(i - LEAD)

    @pl.when(relay)
    def _():
        whole(meta_in, meta_recv).wait()
        told_in = meta_in[...].astype(jnp.float32)
        for u in range(4):
            wanted = jnp.where(row8 < 6, row8 + 8 * u, row8 + 26)
            share[u] = dot(jnp.where(lane8 == wanted, 1.0, 0.0), told_in, NT).astype(jnp.int32)
        goes = share[0, 6:7, :] == target
        jtab[...] = dot(lanef, jnp.where(goes, 1.0, 0.0), NT).astype(jnp.int32)
        to_scalar = pltpu.make_async_copy(jtab, ttab, tab_sem.at[0])
        to_scalar.start()
        to_scalar.wait()
        pltpu.make_async_copy(share.at[0], share_in, share_recv).start()
        for u in range(1, 4):
            remote(share.at[u], share_in, share_send, share_recv, me + u).start()
        whole(piece_in, piece_recv).wait()
        for i in range(N):
            part[i] = piece_in[bounded(ttab[0, i], N)]
        pltpu.make_async_copy(part.at[0], part_in.at[me // 4], part_recv).start()
        for i in range(1, N):
            remote(part.at[i], part_in.at[me // 4], part_send, part_recv, place.target(i)).start()

    for i in range(EARLY, N):
        pack(i + LEAD)
        ship(i)

    whole(share_in, share_recv).wait()
    source = place.all(by_lane[0:1], -1)
    by_step = dot(share_in[...].astype(jnp.float32), jnp.where(rows == source, 1.0, 0.0), NN)
    label0, label1, to1, spares = by_step[0:1], by_step[3:4], by_step[6:7], by_step[7:8]
    goes = to1 == rows.astype(jnp.float32)
    here = jnp.where(to1 == me.astype(jnp.float32), 1.0, 0.0)

    ahead = jnp.where(place.all(by_sublane, -1) < source, 1.0, 0.0)
    group = (rows // G + 1).astype(jnp.float32)
    rank = lax.rem(rows, G).astype(jnp.float32)
    in0, in1 = jnp.where(label0 == group, 1.0, 0.0), jnp.where(label1 == group, 1.0, 0.0)
    passed = dot(in0 + in1, ahead, NN)
    take0 = jnp.where((in0 > 0.5) & (passed == rank), 1.0, 0.0)
    take1 = jnp.where((in1 > 0.5) & (passed + in0 == rank), 1.0, 0.0)

    crowd = jnp.sum(jnp.where(goes, 1.0, 0.0), axis=1, keepdims=True)
    worst = jnp.maximum(jnp.max(crowd, axis=0, keepdims=True), jnp.max(spares, axis=1, keepdims=True))
    facts0 = jnp.where(row8 == 0, by_step[1:2], jnp.where(row8 == 1, by_step[2:3], lanef))
    facts1 = jnp.where(row8 == 0, by_step[4:5], jnp.where(row8 == 1, by_step[5:6], jnp.where(row8 == 2, 1.0 * N, lanef + N)))
    facts = dot(facts0, take0, NT) + dot(facts1, take1, NT)

    flag[...] = jnp.where(worst > 1.5, 1, 0)
    flag_copy = pltpu.make_async_copy(flag, flag_out, in_sem.at[0])
    flag_copy.start()
    same = jnp.where(rows // G == lanes // G, 1.0, 0.0)
    mean = dot(facts, same, NN) * (1.0 / G)
    centred = facts - mean
    spread = jnp.sqrt(dot(centred * centred, same, NN, exact=True) * (1.0 / G))
    adv = centred[0:1] / jnp.maximum(spread[0:1], 1.0)
    count = facts[1:2]
    weight = adv / count
    wrows = jnp.where(row8 == 0, weight, jnp.where((row8 == 1) & (count > 1.5), weight, 0.0))
    by0, by1 = dot(wrows, take0, NN, exact=True), dot(wrows, take1, NN, exact=True)
    wtab[0] = by0
    wtab[1] = jnp.sum(by1 * here, axis=1, keepdims=True) + jnp.zeros((8, N), jnp.float32)
    to_scalar = pltpu.make_async_copy(wtab, wsm, tab_sem.at[1])
    to_scalar.start()
    weights_out[...] = by1
    table_out[...] = jnp.where(row8 == 0, facts[2:3], facts[3:4]).astype(jnp.int32)
    adv_out[...] = adv
    to_scalar.wait()

    def settle(raw, g, _):
        whole(recv.at[pl.ds(0, BATCH)], recv_sem.at[g]).wait()
        for k in range(BATCH):
            i = g * BATCH + k
            row = normed(recv[i], gains) if raw else recv[i]
            rows_out[i] = weighed(row, wsm[0, 0, i], wsm[0, 1, i])
        return 0
    lax.fori_loop(0, RAW // BATCH, functools.partial(settle, True), 0)
    lax.fori_loop(RAW // BATCH, LATE, functools.partial(settle, False), 0)

    whole(part_in, part_recv).wait()
    for t in range(PIECES):
        extra_in[:, pl.ds(t * 128, 128)] = part_in[t]
    rows_out[N] = weighed(extra_in[...], wsm[1, 0, 0], wsm[1, 1, 0])
    lax.fori_loop(LATE, N // BATCH, functools.partial(settle, False), 0)

    whole(send.at[pl.ds(0, N - 1)], send_sem).wait()
    flag_copy.wait()

    @pl.when(relay)
    def _():
        whole(meta.at[pl.ds(0, PIECES - 1)], meta_send).wait()
        whole(piece_in.at[pl.ds(0, PIECES - 1)], piece_send).wait()
        whole(share.at[pl.ds(0, 3)], share_send).wait()
        whole(part.at[pl.ds(0, N - 1)], part_send).wait()

    @pl.when(jnp.logical_not(relay))
    def _():
        whole(meta, meta_send).wait()
        whole(piece_in.at[pl.ds(0, PIECES)], piece_send).wait()


def second(hidden, gain, prompt_of, weights, order, rows_out, hbuf, gbuf, obuf, tab, itab, stab, send, recv, wsm,
           in_sem, tab_sem, send_sem, recv_sem):
    copies = [pltpu.make_async_copy(a, b, in_sem.at[k]) for k, (a, b) in enumerate(
        ((hidden, hbuf), (gain, gbuf), (prompt_of, tab.at[pl.ds(0, 1)]), (weights, wsm), (order, obuf)))]
    for copy in copies:
        copy.start()
    place = Place()
    barrier = place.greet()
    for copy in copies:
        copy.wait()
    rows, lanes = ints((N, N), 0), ints((N, N), 1)
    slot1 = split(tab[0:1] // OWN, place.all(obuf[0:N], 1), jnp.where(rows < lanes, 1.0, 0.0))[1]
    itab[...] = dot(ints((8, N), 1).astype(jnp.float32), slot1, NT).astype(jnp.int32)
    to_scalar = pltpu.make_async_copy(itab, stab, tab_sem)
    to_scalar.start()
    to_scalar.wait()
    pl.semaphore_wait(barrier, N - 1)

    def pack(i, _):
        send[i] = hbuf[bounded(stab[0, i], N)]
        return 0
    lax.fori_loop(0, N, pack, 0)
    pltpu.make_async_copy(send.at[0], recv.at[0], recv_sem).start()

    for i in range(1, N):
        remote(send.at[i], recv.at[i], send_sem, recv_sem, place.target(i)).start()
    whole(recv, recv_sem).wait()
    gains = gbuf[...]

    def settle(i, _):
        rows_out[i] = weighed(normed(recv[i], gains), wsm[0, i], wsm[1, i])
        return 0
    lax.fori_loop(0, N, settle, 0)
    whole(send.at[pl.ds(0, N - 1)], send_sem).wait()


def arrange(table, adv_in, rows_in, out, adv_out, sem, adv_sem):
    put_adv = pltpu.make_async_copy(adv_in, adv_out, adv_sem)
    put_adv.start()
    for q in range(N):
        pltpu.make_async_copy(rows_in.at[bounded(table[0, q], N + 1)], out.at[q], sem).start()
    whole(out, sem).wait()
    put_adv.wait()


def arrange_both(table, adv_in, rows_in, more_in, out, adv_out, sem, adv_sem):
    put_adv = pltpu.make_async_copy(adv_in, adv_out, adv_sem)
    put_adv.start()

    def put(q, _):
        i = bounded(table[1, q], 2 * N)

        @pl.when(i < N)
        def _():
            pltpu.make_async_copy(rows_in.at[i], out.at[q], sem).start()

        @pl.when(i >= N)
        def _():
            pltpu.make_async_copy(more_in.at[i - N], out.at[q], sem).start()
        return 0
    lax.fori_loop(0, N, put, 0)
    whole(out, sem).wait()
    put_adv.wait()


def on_device(hidden, norm_gain, prompt_of, lengths, reward_level):
    count, window, features = hidden.shape
    bf16, f32, i32 = jnp.bfloat16, jnp.float32, jnp.int32
    shape = jax.ShapeDtypeStruct
    any_space = pl.BlockSpec(memory_space=pl.ANY)
    vmem = pl.BlockSpec(memory_space=pltpu.VMEM)
    dma = pltpu.SemaphoreType.DMA
    block = pltpu.VMEM((N, window, features), bf16)
    square, strip = pltpu.VMEM((N, N), i32), pltpu.VMEM((8, N), i32)
    gains = pltpu.VMEM((1, features), f32)
    steps = pltpu.VMEM((N + 8, N), i32)
    order = jnp.asarray(np.concatenate([np.repeat(np.array(ORDER, np.int32)[:, None], N, 1), np.repeat(np.array([ORDER], np.int32), 8, 0)]))
    gain, prompt, length, level = (a.reshape(1, a.shape[0]) for a in (norm_gain, prompt_of, lengths, reward_level))
    rows, table, flag, adv, weights = pl.pallas_call(
        exchange,
        out_shape=(shape((N + 1, window, features), bf16), shape((8, N), i32), shape((1, 1), i32),
                   shape((1, N), f32), shape((8, N), f32)),
        in_specs=[any_space] * 6,
        out_specs=(vmem, vmem, any_space, vmem, vmem),
        scratch_shapes=[
            block, gains, steps, strip, strip, pltpu.SMEM((8, N), i32), strip, pltpu.SMEM((8, N), i32),
            pltpu.VMEM((PIECES, N), i32), square, pltpu.VMEM((4, 8, N), i32), strip,
            pltpu.VMEM((window, features), bf16), pltpu.VMEM((N, window, 128), bf16),
            pltpu.VMEM((N, window, 128), bf16), pltpu.VMEM((PIECES, window, 128), bf16), pltpu.VMEM((window, features), bf16),
            block, block, pltpu.VMEM((2, 8, N), f32), pltpu.SMEM((2, 8, N), f32), pltpu.VMEM((1, 1), i32),
            dma((6,)), dma((2,)), dma, dma, dma, dma, dma, dma, dma, dma, dma, dma((N // BATCH,))],
        compiler_params=pltpu.CompilerParams(collective_id=0, has_side_effects=True),
        name="exchange",
    )(hidden, gain, prompt, length, level, order)

    def put(kernel, *row_blocks):
        return pl.pallas_call(
            kernel,
            out_shape=(shape((N, window, features), bf16), shape((1, N), f32)),
            in_specs=[pl.BlockSpec(memory_space=pltpu.SMEM)] + [any_space] * (1 + len(row_blocks)),
            out_specs=(any_space, any_space),
            scratch_shapes=[dma, dma],
            name=kernel.__name__,
        )(table, adv, *row_blocks)

    def few(_):
        return put(arrange, rows)

    def many(_):
        more = pl.pallas_call(
            second,
            out_shape=shape((N, window, features), bf16),
            in_specs=[any_space] * 5,
            out_specs=vmem,
            scratch_shapes=[
                block, gains, steps, strip, strip, pltpu.SMEM((8, N), i32), block, block, pltpu.SMEM((8, N), f32),
                dma((5,)), dma, dma, dma],
            compiler_params=pltpu.CompilerParams(collective_id=1, has_side_effects=True, vmem_limit_bytes=24 << 20),
            name="second",
        )(hidden, gain, prompt, weights, order)
        return put(arrange_both, rows, more)

    out, adv = lax.switch(flag[0, 0], (few, many), 0)
    return out, adv.reshape(N)


def solution(mesh):
    spec = P(AXES)
    return jax.shard_map(
        on_device, mesh=mesh, in_specs=(P(AXES, None, None), P(), spec, spec, spec),
        out_specs=(P(AXES, None, None), spec), check_vma=False)
```
